256 devices in a mesh: row: 8 (over z_hi, x), col: 32 (over z_lo, y, core).
Axes of the slice: x: 4, y: 4, z: 8 (z_hi: 2, z_lo: 4; z = z_hi * 4 + z_lo), core: 2. Of those that a mesh axis runs over, the one named last changes fastest.
Arguments:
- object_field: float32 [2, 2048, 8192], P(None, 'row', 'col'), may hold values from -6 to 6
- probe: float32 [2, 4, 128, 128], replicated, may hold values from -6 to 6
- patterns: bfloat16 [8, 32, 8, 128, 128], P('row', 'col'), may hold values from 0.5 to 2
- row_scales: float32 [8, 32, 8, 128], P('row', 'col'), may hold values from 0.3 to 3
- positions: int32 [8, 32, 8, 2], P('row', 'col'), may hold values from 0 to 255
- counts: int32 [8, 32], P('row', 'col'), may hold values from 4 to 8, as said below
Outputs:
- object_out: float32 [2, 2048, 8192], P(None, 'row', 'col')
- probe_out: float32 [2, 4, 128, 128], replicated
The draws below stay inside these ranges and needn't reach their ends.
Inputs may be any that keep to these rules, and one draw needn't show every extreme that they name: positions p >= counts[a,b] of tile (a,b) are ignored; some tile has all 8 positions live.
All inputs are finite; a program needn't handle non-finite values.
Results may differ from the reference program's by a relative error of at most 0.0003.
Values sent between devices are 32-bit elements; how exact they have to be, the bound alone decides.
No kernel may reach another device: no remote copies, remote signals or barrier semaphores. Data moves between devices by JAX's collectives and lax.ppermute only.
A program may use at most 128 MiB of HBM per device.

```python
import math
import jax
import jax.numpy as jnp
from jax import lax

PIX = 128
MODES = 4
POS = 8
PASSES = 2
TILE = 256
OBJ_ROWS = 2048
OBJ_COLS = 8192
N_ROW = 8
N_COL = 32


def draw_counts(key, part):
    key_counts, key_full = jax.random.split(key)
    drawn = jax.random.randint(key_counts, (N_ROW * N_COL,), POS // 2, POS + 1)
    chosen = jax.random.randint(key_full, (), 0, N_ROW * N_COL)
    flattened = jnp.where(jnp.arange(N_ROW * N_COL) == chosen, POS, drawn)
    return flattened.reshape(N_ROW, N_COL).astype(jnp.int32)


def touch_ends(values, rng, low, high):
    place = [jax.random.randint(jax.random.fold_in(rng, axis), (), 0, length) for axis, length in enumerate(values.shape)]
    widest = values.shape.index(max(values.shape))
    beside = place[:widest] + [(place[widest] + 1) % values.shape[widest]] + place[widest + 1:]
    return values.at[tuple(place)].set(low).at[tuple(beside)].set(high)


def block_scale(rng, shape, pieces, low, high):
    def one(axis_at, shards_of):
        heights = jax.random.uniform(jax.random.fold_in(jax.random.fold_in(rng, 6), axis_at), (shards_of,), jnp.float32, low / len(pieces), high / len(pieces))
        return jnp.repeat(jnp.exp(heights), shape[axis_at] // shards_of).reshape((-1,) + (1,) * (len(shape) - axis_at - 1))

    level = one(*pieces[0])
    for cut in pieces[1:]:
        level = level * one(*cut)
    return level


def bell_draw(key, dims, deviation, limit, shards=(), kind=jnp.bfloat16):
    loudness = block_scale(key, dims, shards, -0.22, 0.18) if shards else 1.0
    entries = jax.random.normal(key, dims, jnp.float32) * deviation * loudness
    return jnp.minimum(jnp.maximum(entries, -limit), limit).astype(kind)


def setup_inputs(seed: int = 0) -> dict:
    streams_of = jax.random.split(jax.random.key(seed), 7)
    return {
        "object_field": bell_draw(streams_of[0], (2, OBJ_ROWS, OBJ_COLS), 1.0, 6.0, ((1, 8), (2, 32)), jnp.float32),
        "probe": bell_draw(streams_of[1], (2, MODES, PIX, PIX), 1.0, 6.0, (), jnp.float32),
        "patterns": jnp.clip(0.5 + 1.5 * jax.random.uniform(streams_of[2], (N_ROW, N_COL, POS, PIX, PIX), jnp.float32) ** block_scale(streams_of[2], (N_ROW, N_COL, POS, PIX, PIX), ((0, 8), (1, 32)), -0.2, 0.2), 0.5, 2.0).astype(jnp.bfloat16),
        "row_scales": jnp.clip(jnp.exp(math.log(3.0) - 2.3025851 * jax.random.uniform(streams_of[3], (N_ROW, N_COL, POS, PIX), jnp.float32) ** block_scale(streams_of[3], (N_ROW, N_COL, POS, PIX), ((0, 8), (1, 32)), -0.2, 0.2)), 0.3, 3.0),
        "positions": touch_ends(jax.random.randint(streams_of[4], (N_ROW, N_COL, POS, 2), 0, TILE), jax.random.fold_in(streams_of[4], 1), 0, TILE - 1).astype(jnp.int32),
        "counts": draw_counts(jax.random.fold_in(streams_of[6], 71), 0),
    }


def reference(object_field, probe, patterns, row_scales, positions, counts):
    half_width = PIX // 2
    object_now = object_field[0] + 1j * object_field[1]
    probe_now = probe[0] + 1j * probe[1]
    amplitudes = (patterns.astype(jnp.float32) * row_scales[..., None]).reshape(-1, PIX, PIX)
    tile_rows = jnp.broadcast_to((jnp.arange(N_ROW, dtype=jnp.int32) * TILE)[:, None, None], (N_ROW, N_COL, POS))
    tile_cols = jnp.broadcast_to((jnp.arange(N_COL, dtype=jnp.int32) * TILE)[None, :, None], (N_ROW, N_COL, POS))
    row_starts = (tile_rows + positions[..., 0]).reshape(-1).astype(jnp.int32)
    col_starts = (tile_cols + positions[..., 1]).reshape(-1).astype(jnp.int32)
    live_flag = (jnp.arange(POS, dtype=jnp.int32)[None, None, :] < counts[:, :, None]).astype(object_field.dtype).reshape(-1)
    for pass_number in range(PASSES):
        padded = jnp.pad(object_now, half_width)

        def one_position(running, element):
            updates, gradient, weight = running
            row_at, col_at, live_now, amplitude = element
            object_patch = lax.dynamic_slice(padded, (row_at, col_at), (PIX, PIX))
            exit_wave = probe_now * object_patch[None]
            far_field = jnp.fft.fft2(exit_wave, norm='ortho')
            intensity = lax.optimization_barrier(jnp.sum(jnp.real(far_field) ** 2 + jnp.imag(far_field) ** 2, axis=0))
            factor = amplitude / jnp.maximum(jnp.sqrt(intensity), 0.5)
            back_wave = jnp.fft.ifft2(far_field * factor[None], norm='ortho')
            difference = (back_wave - exit_wave) * live_now
            contribution = lax.optimization_barrier(jnp.sum(jnp.conj(probe_now) * difference, axis=0))
            current = lax.dynamic_slice(updates, (row_at, col_at), (PIX, PIX))
            updates = lax.dynamic_update_slice(updates, current + contribution, (row_at, col_at))
            gradient = gradient + jnp.conj(object_patch)[None] * difference
            weight = weight + live_now * (jnp.real(object_patch) ** 2 + jnp.imag(object_patch) ** 2)
            return ((updates, gradient, weight), None)
        initial = (jnp.zeros_like(padded), jnp.zeros_like(probe_now), jnp.zeros((PIX, PIX), object_field.dtype))
        (updates, gradient, weight), unused = lax.scan(one_position, initial, (row_starts, col_starts, live_flag, amplitudes))
        probe_peak = jnp.max(lax.optimization_barrier(jnp.sum(jnp.real(probe_now) ** 2 + jnp.imag(probe_now) ** 2, axis=0)))
        object_now = object_now + updates[half_width:-half_width, half_width:-half_width] / probe_peak
        probe_now = probe_now + gradient / weight[None]
    object_out = jnp.stack([jnp.real(object_now), jnp.imag(object_now)])
    probe_out = jnp.stack([jnp.real(probe_now), jnp.imag(probe_now)])
    return (object_out, probe_out)
```

```python
import functools

import numpy as np

import jax
import jax.numpy as jnp
from jax import lax
from jax.experimental import pallas as pl
from jax.experimental.pallas import tpu as pltpu
from jax.sharding import PartitionSpec as P

LANES = 128
SUBLANES = 8


def dft_tables(length):
    index = np.arange(length)
    angle = (np.outer(index, index) % length) * (2.0 * np.pi / length)
    cosine = np.cos(angle) / np.sqrt(length)
    sine = np.sin(angle) / np.sqrt(length)
    forward = np.block([[cosine, -sine], [sine, cosine]]).astype(np.float32)
    high = forward.astype(jnp.bfloat16)
    low = (forward - high.astype(np.float32)).astype(jnp.bfloat16)
    return high, low, np.ascontiguousarray(high.T), np.ascontiguousarray(low.T)


def split(value):
    high = value.astype(jnp.bfloat16)
    low = (value - high.astype(jnp.float32)).astype(jnp.bfloat16)
    return high, low


def mm(left, right):
    return jnp.dot(left, right, preferred_element_type=jnp.float32)


def product(left, right):
    (lh, ll), (rh, rl) = left, right
    return mm(lh, rh) + (mm(lh, rl) + mm(ll, rh))


def pass_kernel(
    starts, counts, frame, probe, amplitude, fh, fl, ih, il, updates, sums, *, modes, size, margin
):
    updates[...] = jnp.zeros_like(updates)
    sums[...] = jnp.zeros_like(sums)
    forward = (fh[...], fl[...])
    inverse = (ih[...], il[...])

    def position(p, carry):
        row = starts[p, 0]
        col = starts[p, 1] + margin
        base = pl.multiple_of(col // LANES * LANES, LANES)
        shift = col % LANES
        tall, wide = size + SUBLANES, 2 * size
        down = row % SUBLANES
        rows = pl.ds(pl.multiple_of(row // SUBLANES * SUBLANES, SUBLANES), tall)
        cols = pl.ds(base, wide)

        def cut(window):
            window = pltpu.roll(window, lax.rem(wide - shift, wide), 1)[:, :size]
            return pltpu.roll(window, lax.rem(tall - down, tall), 0)[:size]

        def placed(patch):
            patch = jnp.concatenate([patch, jnp.zeros((SUBLANES, size), jnp.float32)], axis=0)
            patch = pltpu.roll(patch, down, 0)
            return pltpu.roll(jnp.concatenate([patch, jnp.zeros_like(patch)], axis=1), shift, 1)

        patch_re = cut(frame[0, rows, cols])
        patch_im = cut(frame[1, rows, cols])
        waves = []
        for m in range(modes):
            pr, pi = probe[0, m], probe[1, m]
            waves.append((pr * patch_re - pi * patch_im, pr * patch_im + pi * patch_re))
        stacked = jnp.concatenate([jnp.concatenate(w, axis=1) for w in waves], axis=0)
        half = product(split(stacked), forward)
        blocks = [half[m * size : (m + 1) * size] for m in range(modes)]
        side = jnp.concatenate(
            [jnp.concatenate([b[:, :size], b[:, size:]], axis=0) for b in blocks], axis=1
        )
        far = product(inverse, split(side))
        squares = far * far
        power = squares[:size] + squares[size:]
        intensity = power[:, :size]
        for m in range(1, modes):
            intensity = intensity + power[:, m * size : (m + 1) * size]
        factor = amplitude[p] / jnp.maximum(jnp.sqrt(intensity), 0.5)
        wide = jnp.concatenate([factor] * modes, axis=1)
        scaled = far * jnp.concatenate([wide, wide], axis=0)
        half = product(forward, split(scaled))
        stacked = jnp.concatenate(
            [
                jnp.concatenate(
                    [half[:size, m * size : (m + 1) * size], half[size:, m * size : (m + 1) * size]],
                    axis=1,
                )
                for m in range(modes)
            ],
            axis=0,
        )
        back = product(split(stacked), inverse)
        total_re = total_im = None
        for m in range(modes):
            pr, pi = probe[0, m], probe[1, m]
            dr = back[m * size : (m + 1) * size, :size] - waves[m][0]
            di = back[m * size : (m + 1) * size, size:] - waves[m][1]
            sums[m] += patch_re * dr + patch_im * di
            sums[modes + m] += patch_re * di - patch_im * dr
            add_re = pr * dr + pi * di
            add_im = pr * di - pi * dr
            total_re = add_re if m == 0 else total_re + add_re
            total_im = add_im if m == 0 else total_im + add_im
        sums[2 * modes] += patch_re * patch_re + patch_im * patch_im
        updates[0, rows, cols] += placed(total_re)
        updates[1, rows, cols] += placed(total_im)
        return carry

    lax.fori_loop(0, counts[0], position, 0)
    strength = probe[0, 0] * probe[0, 0] + probe[1, 0] * probe[1, 0]
    for m in range(1, modes):
        strength = strength + probe[0, m] * probe[0, m] + probe[1, m] * probe[1, m]
    updates[...] = updates[...] / jnp.max(strength)


def run_pass(starts, count, frame, probe, amplitude, tables, margin):
    modes, size = probe.shape[1], probe.shape[2]
    vmem = pl.BlockSpec(memory_space=pltpu.VMEM)
    smem = pl.BlockSpec(memory_space=pltpu.SMEM)
    flops = 24 * starts.shape[0] * modes * size * (2 * size) ** 2
    return pl.pallas_call(
        functools.partial(pass_kernel, modes=modes, size=size, margin=margin),
        out_shape=(
            jax.ShapeDtypeStruct(frame.shape, jnp.float32),
            jax.ShapeDtypeStruct((2 * modes + 1, size, size), jnp.float32),
        ),
        in_specs=[smem, smem] + [vmem] * 7,
        out_specs=(vmem, vmem),
        cost_estimate=pl.CostEstimate(flops=flops, bytes_accessed=6 << 20, transcendentals=0),
        compiler_params=pltpu.CompilerParams(vmem_limit_bytes=48 << 20),
    )(starts, count, frame, probe, amplitude, *tables)


def neighbours(low_strip, high_strip, axis):
    count = lax.axis_size(axis)
    up = [(i, i + 1) for i in range(count - 1)]
    down = [(i + 1, i) for i in range(count - 1)]
    return lax.ppermute(high_strip, axis, up), lax.ppermute(low_strip, axis, down)


def spread(chunk, axis):
    count = lax.axis_size(axis)
    return lax.all_to_all(jnp.broadcast_to(chunk[None], (count, *chunk.shape)), axis, 0, 0, tiled=True)


def total(sums):
    count = lax.axis_size("col")
    parts = lax.all_to_all(sums.reshape(count, -1, LANES), "col", 0, 0, tiled=True)
    part = jnp.sum(spread(jnp.sum(parts, axis=0), "row"), axis=0)
    return spread(part, "col").reshape(sums.shape)


def at(array, dim, start, stop):
    return lax.slice_in_dim(array, start, stop, axis=dim)


def padded(array, dim, low, size):
    pads = [(0, 0, 0)] * array.ndim
    pads[dim] = (low, size - low - array.shape[dim], 0)
    return lax.pad(array, jnp.float32(0), pads)


def on_device(object_field, probe, patterns, row_scales, positions, counts):
    modes, size = probe.shape[1], probe.shape[2]
    rim = size // 2
    rows, cols = object_field.shape[1:]
    tall, wide = rows + 2 * rim, cols + 2 * LANES
    margin = LANES - rim
    tables = [jnp.asarray(t) for t in dft_tables(size)]
    amplitude = patterns[0, 0].astype(jnp.float32) * row_scales[0, 0][..., None]
    starts, count = positions[0, 0], counts[0]

    low, high = neighbours(at(object_field, 1, 0, rim), at(object_field, 1, rows - rim, rows), "row")
    frame = jnp.concatenate([low, object_field, high], axis=1)
    low, high = neighbours(at(frame, 2, 0, LANES), at(frame, 2, cols - LANES, cols), "col")
    frame = jnp.concatenate([low, frame, high], axis=2)

    updates, sums = run_pass(starts, count, frame, probe, amplitude, tables, margin)
    low, high = neighbours(at(updates, 1, 0, 2 * rim), at(updates, 1, rows, tall), "row")
    updates = updates + padded(low, 1, 0, tall) + padded(high, 1, rows, tall)
    left = margin, margin + 2 * rim
    right = margin + cols, margin + cols + 2 * rim
    low, high = neighbours(at(updates, 2, *left), at(updates, 2, *right), "col")
    updates = updates + padded(low, 2, margin, wide) + padded(high, 2, margin + cols, wide)
    at_row = lax.broadcasted_iota(jnp.int32, (1, tall, 1), 1) + (lax.axis_index("row") * rows - rim)
    at_col = lax.broadcasted_iota(jnp.int32, (1, 1, wide), 2) + (lax.axis_index("col") * cols - LANES)
    inside = (at_row >= 0) & (at_row < rows * lax.axis_size("row"))
    inside = inside & (at_col >= 0) & (at_col < cols * lax.axis_size("col"))
    frame = frame + jnp.where(inside, updates, 0.0)
    sums = total(sums)
    probe = probe + sums[: 2 * modes].reshape(probe.shape) / sums[2 * modes]

    updates, sums = run_pass(starts, count, frame, probe, amplitude, tables, margin)
    low, high = neighbours(at(updates, 1, 0, rim), at(updates, 1, tall - rim, tall), "row")
    middle = at(updates, 1, rim, rim + rows)
    middle = middle + padded(low, 1, 0, rows) + padded(high, 1, rows - rim, rows)
    low, high = neighbours(
        at(middle, 2, margin, LANES), at(middle, 2, LANES + cols, wide - margin), "col"
    )
    tile = at(middle, 2, LANES, LANES + cols)
    tile = tile + padded(low, 2, 0, cols) + padded(high, 2, cols - rim, cols)
    object_out = frame[:, rim : rim + rows, LANES : LANES + cols] + tile
    sums = total(sums)
    probe_out = probe + sums[: 2 * modes].reshape(probe.shape) / sums[2 * modes]
    return object_out, probe_out


def solution(mesh):
    placed = (
        P(None, "row", "col"),
        P(),
        P("row", "col", None, None, None),
        P("row", "col", None, None),
        P("row", "col", None, None),
        P("row", "col"),
    )
    return jax.shard_map(
        on_device,
        mesh=mesh,
        in_specs=placed,
        out_specs=(P(None, "row", "col"), P()),
        check_vma=False,
    )
```

```python
import functools

import numpy as np

import jax
import jax.numpy as jnp
from jax import lax
from jax.experimental import pallas as pl
from jax.experimental.pallas import tpu as pltpu
from jax.sharding import PartitionSpec as P

LANES = 128
SUBLANES = 8
CORES = 2


def dft_tables(length):
    index = np.arange(length)
    angle = (np.outer(index, index) % length) * (2.0 * np.pi / length)
    cosine = np.cos(angle) / np.sqrt(length)
    sine = np.sin(angle) / np.sqrt(length)
    forward = np.block([[cosine, -sine], [sine, cosine]]).astype(np.float32)
    high = forward.astype(jnp.bfloat16)
    low = (forward - high.astype(np.float32)).astype(jnp.bfloat16)
    return high, low, np.ascontiguousarray(high.T), np.ascontiguousarray(low.T)


def split(value):
    high = value.astype(jnp.bfloat16)
    low = (value - high.astype(jnp.float32)).astype(jnp.bfloat16)
    return high, low


def mm(left, right):
    return jnp.dot(left, right, preferred_element_type=jnp.float32)


def product(left, right):
    (lh, ll), (rh, rl) = left, right
    return mm(lh, rh) + (mm(lh, rl) + mm(ll, rh))


def pass_kernel(*refs, modes, size, margin, renew):
    if renew:
        starts, counts, core, frame, old_probe, mean_mine, mean_other, amplitude, *refs = refs
        fh, fl, ih, il, updates, mine, other, probe, sums = refs
        half_rows = mean_mine.shape[0]
        sums[pl.ds(pl.multiple_of(core[0] * half_rows, size), half_rows)] = mean_mine[...]
        sums[pl.ds(pl.multiple_of((1 - core[0]) * half_rows, size), half_rows)] = mean_other[...]
        weight = sums[pl.ds(2 * modes * size, size)]
        for part in range(2):
            for m in range(modes):
                step = sums[pl.ds((part * modes + m) * size, size)] / weight
                probe[part, m] = old_probe[part, m] + step
    else:
        starts, counts, core, frame, probe, amplitude, *refs = refs
        fh, fl, ih, il, updates, mine, other, sums = refs
    updates[...] = jnp.zeros_like(updates)
    sums[...] = jnp.zeros_like(sums)
    forward = (fh[...], fl[...])
    inverse = (ih[...], il[...])

    def position(p, carry):
        row = starts[p, 0]
        col = starts[p, 1] + margin
        base = pl.multiple_of(col // LANES * LANES, LANES)
        shift = col % LANES
        tall, wide = size + SUBLANES, 2 * size
        down = row % SUBLANES
        rows = pl.ds(pl.multiple_of(row // SUBLANES * SUBLANES, SUBLANES), tall)
        cols = pl.ds(base, wide)

        def cut(window):
            window = pltpu.roll(window, lax.rem(wide - shift, wide), 1)[:, :size]
            return pltpu.roll(window, lax.rem(tall - down, tall), 0)[:size]

        def placed(patch):
            patch = jnp.concatenate([patch, jnp.zeros((SUBLANES, size), jnp.float32)], axis=0)
            patch = pltpu.roll(patch, down, 0)
            return pltpu.roll(jnp.concatenate([patch, jnp.zeros_like(patch)], axis=1), shift, 1)

        patch_re = cut(frame[0, rows, cols])
        patch_im = cut(frame[1, rows, cols])
        waves = []
        for m in range(modes):
            pr, pi = probe[0, m], probe[1, m]
            waves.append((pr * patch_re - pi * patch_im, pr * patch_im + pi * patch_re))
        stacked = jnp.concatenate([jnp.concatenate(w, axis=1) for w in waves], axis=0)
        half = product(split(stacked), forward)
        blocks = [half[m * size : (m + 1) * size] for m in range(modes)]
        side = jnp.concatenate(
            [jnp.concatenate([b[:, :size], b[:, size:]], axis=0) for b in blocks], axis=1
        )
        far = product(inverse, split(side))
        squares = far * far
        power = squares[:size] + squares[size:]
        intensity = power[:, :size]
        for m in range(1, modes):
            intensity = intensity + power[:, m * size : (m + 1) * size]
        factor = amplitude[p] / jnp.maximum(jnp.sqrt(intensity), 0.5)
        wide = jnp.concatenate([factor] * modes, axis=1)
        scaled = far * jnp.concatenate([wide, wide], axis=0)
        half = product(forward, split(scaled))
        stacked = jnp.concatenate(
            [
                jnp.concatenate(
                    [half[:size, m * size : (m + 1) * size], half[size:, m * size : (m + 1) * size]],
                    axis=1,
                )
                for m in range(modes)
            ],
            axis=0,
        )
        back = product(split(stacked), inverse)
        total_re = total_im = None
        for m in range(modes):
            pr, pi = probe[0, m], probe[1, m]
            dr = back[m * size : (m + 1) * size, :size] - waves[m][0]
            di = back[m * size : (m + 1) * size, size:] - waves[m][1]
            sums[pl.ds(m * size, size)] += patch_re * dr + patch_im * di
            sums[pl.ds((modes + m) * size, size)] += patch_re * di - patch_im * dr
            add_re = pr * dr + pi * di
            add_im = pr * di - pi * dr
            total_re = add_re if m == 0 else total_re + add_re
            total_im = add_im if m == 0 else total_im + add_im
        sums[pl.ds(2 * modes * size, size)] += patch_re * patch_re + patch_im * patch_im
        updates[0, rows, cols] += placed(total_re)
        updates[1, rows, cols] += placed(total_im)
        return carry

    lax.fori_loop(0, counts[0], position, 0)
    strength = probe[0, 0] * probe[0, 0] + probe[1, 0] * probe[1, 0]
    for m in range(1, modes):
        strength = strength + probe[0, m] * probe[0, m] + probe[1, m] * probe[1, m]
    updates[...] = updates[...] / jnp.max(strength)
    half_rows = mine.shape[0]
    mine[...] = sums[pl.ds(pl.multiple_of(core[0] * half_rows, size), half_rows)]
    other[...] = sums[pl.ds(pl.multiple_of((1 - core[0]) * half_rows, size), half_rows)]


def run_pass(starts, count, core, frame, probe, means, amplitude, tables, margin):
    modes, size = probe.shape[1], probe.shape[2]
    renew = means is not None
    half_rows = (modes + 1) * size
    vmem = pl.BlockSpec(memory_space=pltpu.VMEM)
    smem = pl.BlockSpec(memory_space=pltpu.SMEM)
    flops = 24 * starts.shape[0] * modes * size * (2 * size) ** 2
    half = jax.ShapeDtypeStruct((half_rows, size), jnp.float32)
    shapes = [jax.ShapeDtypeStruct(frame.shape, jnp.float32), half, half]
    if renew:
        shapes.append(jax.ShapeDtypeStruct(probe.shape, jnp.float32))
    operands = [frame, probe, *(means or ()), amplitude, *tables]
    return pl.pallas_call(
        functools.partial(pass_kernel, modes=modes, size=size, margin=margin, renew=renew),
        out_shape=shapes,
        in_specs=[smem] * 3 + [vmem] * len(operands),
        out_specs=[vmem] * len(shapes),
        scratch_shapes=[pltpu.VMEM((2 * half_rows, size), jnp.float32)],
        cost_estimate=pl.CostEstimate(flops=flops, bytes_accessed=6 << 20, transcendentals=0),
        compiler_params=pltpu.CompilerParams(vmem_limit_bytes=48 << 20),
    )(starts, count, core, *operands)


def neighbours(low_strip, high_strip, axis):
    count = lax.axis_size(axis)
    up = [(i, i + 1) for i in range(count - 1)]
    down = [(i + 1, i) for i in range(count - 1)]
    return lax.ppermute(high_strip, axis, up), lax.ppermute(low_strip, axis, down)


AXES = ("row", "col")


def groups(row_step, col_step):
    n_row, n_col = lax.axis_size("row"), lax.axis_size("col")

    def flat(zh, x, zl, yc):
        return (zh * row_step + x) * n_col + zl * col_step + yc

    z = [(zh, zl) for zh in range(n_row // row_step) for zl in range(n_col // col_step)]
    planes = [
        [flat(zh, x, zl, y * CORES + c) for x in range(row_step) for y in range(col_step // CORES)]
        for zh, zl in z
        for c in range(CORES)
    ]
    lines = [[flat(zh, x, zl, yc) for zh, zl in z] for x in range(row_step) for yc in range(col_step)]
    return planes, lines


def exchange(blocks, members):
    return lax.all_to_all(blocks, AXES, 0, 0, axis_index_groups=members, tiled=True)


def spread(chunk, members):
    return exchange(jnp.broadcast_to(chunk[None], (len(members[0]), *chunk.shape)), members)


def swap(block):
    count = lax.axis_size("col")
    return lax.ppermute(block, "col", [(i, i ^ 1) for i in range(count)])


def total(mine, other):
    planes, lines = groups(4, 8)
    mine = mine + swap(other)
    parts = exchange(mine.reshape(len(planes[0]), -1, LANES), planes)
    part = jnp.sum(spread(jnp.sum(parts, axis=0), lines), axis=0)
    mine = spread(part, planes).reshape(mine.shape)
    return mine, swap(mine)


def at(array, dim, start, stop):
    return lax.slice_in_dim(array, start, stop, axis=dim)


def padded(array, dim, low, size):
    pads = [(0, 0, 0)] * array.ndim
    pads[dim] = (low, size - low - array.shape[dim], 0)
    return lax.pad(array, jnp.float32(0), pads)


def on_device(object_field, probe, patterns, row_scales, positions, counts):
    modes, size = probe.shape[1], probe.shape[2]
    rim = size // 2
    rows, cols = object_field.shape[1:]
    tall, wide = rows + 2 * rim, cols + 2 * LANES
    margin = LANES - rim
    tables = [jnp.asarray(t) for t in dft_tables(size)]
    amplitude = patterns[0, 0].astype(jnp.float32) * row_scales[0, 0][..., None]
    starts, count = positions[0, 0], counts[0]

    low, high = neighbours(at(object_field, 1, 0, rim), at(object_field, 1, rows - rim, rows), "row")
    frame = jnp.concatenate([low, object_field, high], axis=1)
    low, high = neighbours(at(frame, 2, 0, LANES), at(frame, 2, cols - LANES, cols), "col")
    frame = jnp.concatenate([low, frame, high], axis=2)

    core = (lax.axis_index("col") % CORES).reshape(1)
    left, right = margin, LANES + cols + rim
    updates, mine, other = run_pass(starts, count, core, frame, probe, None, amplitude, tables, margin)
    means = total(mine, other)
    strips = at(updates, 2, left, right)
    low, high = neighbours(at(strips, 1, 0, 2 * rim), at(strips, 1, rows, tall), "row")
    strips = strips + padded(low, 1, 0, tall) + padded(high, 1, rows, tall)
    low, high = neighbours(at(strips, 2, 0, 2 * rim), at(strips, 2, cols, cols + 2 * rim), "col")
    strips = strips + padded(low, 2, 0, cols + 2 * rim) + padded(high, 2, cols, cols + 2 * rim)
    updates = padded(strips, 2, left, wide)
    at_row = lax.broadcasted_iota(jnp.int32, (1, tall, 1), 1) + (lax.axis_index("row") * rows - rim)
    at_col = lax.broadcasted_iota(jnp.int32, (1, 1, wide), 2) + (lax.axis_index("col") * cols - LANES)
    inside = (at_row >= 0) & (at_row < rows * lax.axis_size("row"))
    inside = inside & (at_col >= 0) & (at_col < cols * lax.axis_size("col"))
    frame = frame + jnp.where(inside, updates, 0.0)

    updates, mine, other, probe = run_pass(
        starts, count, core, frame, probe, means, amplitude, tables, margin
    )
    mine, other = total(mine, other)
    low, high = neighbours(
        at(at(updates, 1, 0, rim), 2, left, right), at(at(updates, 1, tall - rim, tall), 2, left, right), "row"
    )
    middle = at(at(updates, 1, rim, rim + rows), 2, left, right)
    middle = middle + padded(low, 1, 0, rows) + padded(high, 1, rows - rim, rows)
    low, high = neighbours(at(middle, 2, 0, rim), at(middle, 2, rim + cols, cols + 2 * rim), "col")
    tile = at(middle, 2, rim, rim + cols)
    tile = tile + padded(low, 2, 0, cols) + padded(high, 2, cols - rim, cols)
    object_out = frame[:, rim : rim + rows, LANES : LANES + cols] + tile
    lower = jnp.where(core[0] == 0, mine, other)
    upper = jnp.where(core[0] == 0, other, mine)
    sums = jnp.concatenate([lower, upper]).reshape(-1, size, size)
    probe_out = probe + sums[: 2 * modes].reshape(probe.shape) / sums[2 * modes]
    return object_out, probe_out


def solution(mesh):
    placed = (
        P(None, "row", "col"),
        P(),
        P("row", "col", None, None, None),
        P("row", "col", None, None),
        P("row", "col", None, None),
        P("row", "col"),
    )
    return jax.shard_map(
        on_device,
        mesh=mesh,
        in_specs=placed,
        out_specs=(P(None, "row", "col"), P()),
        check_vma=False,
    )
```

```python
import functools

import numpy as np

import jax
import jax.numpy as jnp
from jax import lax
from jax.experimental import pallas as pl
from jax.experimental.pallas import tpu as pltpu
from jax.sharding import PartitionSpec as P


LANES = 128
SUBLANES = 8
CORES = 2


def dft_tables(length):
    index = np.arange(length)
    angle = (np.outer(index, index) % length) * (2.0 * np.pi / length)
    cosine = np.cos(angle) / np.sqrt(length)
    sine = np.sin(angle) / np.sqrt(length)
    forward = np.block([[cosine, -sine], [sine, cosine]]).astype(np.float32)
    high = forward.astype(jnp.bfloat16)
    low = (forward - high.astype(np.float32)).astype(jnp.bfloat16)
    return high, low, np.ascontiguousarray(high.T), np.ascontiguousarray(low.T)


def split(value):
    high = value.astype(jnp.bfloat16)
    low = (value - high.astype(jnp.float32)).astype(jnp.bfloat16)
    return high, low


def mm(left, right):
    return jnp.dot(left, right, preferred_element_type=jnp.float32)


def product(left, right):
    (lh, ll), (rh, rl) = left, right
    return mm(lh, rh) + (mm(lh, rl) + mm(ll, rh))


def pass_kernel(*refs, modes, size, margin, renew):
    if renew:
        starts, counts, core, frame, old_probe, mean_mine, mean_other, amplitude, *refs = refs
        fh, fl, ih, il, updates, mine, other, probe, sums = refs
        half_rows = mean_mine.shape[0]
        sums[pl.ds(pl.multiple_of(core[0] * half_rows, size), half_rows)] = mean_mine[...]
        sums[pl.ds(pl.multiple_of((1 - core[0]) * half_rows, size), half_rows)] = mean_other[...]
        weight = sums[pl.ds(2 * modes * size, size)]
        for part in range(2):
            for m in range(modes):
                step = sums[pl.ds((part * modes + m) * size, size)] / weight
                probe[part, m] = old_probe[part, m] + step
    else:
        starts, counts, core, frame, probe, amplitude, *refs = refs
        fh, fl, ih, il, updates, mine, other, sums = refs
    updates[...] = jnp.zeros_like(updates)
    sums[...] = jnp.zeros_like(sums)
    forward = (fh[...], fl[...])
    inverse = (ih[...], il[...])

    def position(p, carry):
        row = starts[p, 0]
        col = starts[p, 1] + margin
        base = pl.multiple_of(col // LANES * LANES, LANES)
        shift = col % LANES
        tall, wide = size + SUBLANES, 2 * size
        down = row % SUBLANES
        rows = pl.ds(pl.multiple_of(row // SUBLANES * SUBLANES, SUBLANES), tall)
        cols = pl.ds(base, wide)

        def cut(window):
            window = pltpu.roll(window, lax.rem(wide - shift, wide), 1)[:, :size]
            return pltpu.roll(window, lax.rem(tall - down, tall), 0)[:size]

        def placed(patch):
            patch = jnp.concatenate([patch, jnp.zeros((SUBLANES, size), jnp.float32)], axis=0)
            patch = pltpu.roll(patch, down, 0)
            return pltpu.roll(jnp.concatenate([patch, jnp.zeros_like(patch)], axis=1), shift, 1)

        patch_re = cut(frame[0, rows, cols])
        patch_im = cut(frame[1, rows, cols])
        waves = []
        for m in range(modes):
            pr, pi = probe[0, m], probe[1, m]
            waves.append((pr * patch_re - pi * patch_im, pr * patch_im + pi * patch_re))
        stacked = jnp.concatenate([jnp.concatenate(w, axis=1) for w in waves], axis=0)
        half = product(split(stacked), forward)
        blocks = [half[m * size : (m + 1) * size] for m in range(modes)]
        side = jnp.concatenate(
            [jnp.concatenate([b[:, :size], b[:, size:]], axis=0) for b in blocks], axis=1
        )
        far = product(inverse, split(side))
        squares = far * far
        power = squares[:size] + squares[size:]
        intensity = power[:, :size]
        for m in range(1, modes):
            intensity = intensity + power[:, m * size : (m + 1) * size]
        factor = amplitude[p] / jnp.maximum(jnp.sqrt(intensity), 0.5)
        wide = jnp.concatenate([factor] * modes, axis=1)
        scaled = far * jnp.concatenate([wide, wide], axis=0)
        half = product(forward, split(scaled))
        stacked = jnp.concatenate(
            [
                jnp.concatenate(
                    [half[:size, m * size : (m + 1) * size], half[size:, m * size : (m + 1) * size]],
                    axis=1,
                )
                for m in range(modes)
            ],
            axis=0,
        )
        back = product(split(stacked), inverse)
        total_re = total_im = None
        for m in range(modes):
            pr, pi = probe[0, m], probe[1, m]
            dr = back[m * size : (m + 1) * size, :size] - waves[m][0]
            di = back[m * size : (m + 1) * size, size:] - waves[m][1]
            sums[pl.ds(m * size, size)] += patch_re * dr + patch_im * di
            sums[pl.ds((modes + m) * size, size)] += patch_re * di - patch_im * dr
            add_re = pr * dr + pi * di
            add_im = pr * di - pi * dr
            total_re = add_re if m == 0 else total_re + add_re
            total_im = add_im if m == 0 else total_im + add_im
        sums[pl.ds(2 * modes * size, size)] += patch_re * patch_re + patch_im * patch_im
        updates[0, rows, cols] += placed(total_re)
        updates[1, rows, cols] += placed(total_im)
        return carry

    lax.fori_loop(0, counts[0], position, 0)
    strength = probe[0, 0] * probe[0, 0] + probe[1, 0] * probe[1, 0]
    for m in range(1, modes):
        strength = strength + probe[0, m] * probe[0, m] + probe[1, m] * probe[1, m]
    updates[...] = updates[...] / jnp.max(strength)
    half_rows = mine.shape[0]
    mine[...] = sums[pl.ds(pl.multiple_of(core[0] * half_rows, size), half_rows)]
    other[...] = sums[pl.ds(pl.multiple_of((1 - core[0]) * half_rows, size), half_rows)]


def run_pass(starts, count, core, frame, probe, means, amplitude, tables, margin):
    modes, size = probe.shape[1], probe.shape[2]
    renew = means is not None
    half_rows = (modes + 1) * size
    vmem = pl.BlockSpec(memory_space=pltpu.VMEM)
    smem = pl.BlockSpec(memory_space=pltpu.SMEM)
    flops = 24 * starts.shape[0] * modes * size * (2 * size) ** 2
    half = jax.ShapeDtypeStruct((half_rows, size), jnp.float32)
    shapes = [jax.ShapeDtypeStruct(frame.shape, jnp.float32), half, half]
    if renew:
        shapes.append(jax.ShapeDtypeStruct(probe.shape, jnp.float32))
    operands = [frame, probe, *(means or ()), amplitude, *tables]
    return pl.pallas_call(
        functools.partial(pass_kernel, modes=modes, size=size, margin=margin, renew=renew),
        out_shape=shapes,
        in_specs=[smem] * 3 + [vmem] * len(operands),
        out_specs=[vmem] * len(shapes),
        scratch_shapes=[pltpu.VMEM((2 * half_rows, size), jnp.float32)],
        cost_estimate=pl.CostEstimate(flops=flops, bytes_accessed=6 << 20, transcendentals=0),
        compiler_params=pltpu.CompilerParams(vmem_limit_bytes=48 << 20),
    )(starts, count, core, *operands)


def neighbours(low_strip, high_strip, axis):
    count = lax.axis_size(axis)
    odd = lax.axis_index(axis) % 2 == 1

    def meet(block, start):
        pairs = [(i, i + 1) for i in range(start, count - 1, 2)]
        return lax.ppermute(block, axis, pairs + [(j, i) for i, j in pairs])

    first = meet(jnp.where(odd, high_strip, low_strip), 1)
    second = meet(jnp.where(odd, low_strip, high_strip), 0)
    return jnp.where(odd, second, first), jnp.where(odd, first, second)


AXES = ("row", "col")


def groups(row_step, col_step):
    n_row, n_col = lax.axis_size("row"), lax.axis_size("col")

    def flat(zh, x, zl, yc):
        return (zh * row_step + x) * n_col + zl * col_step + yc

    z = [(zh, zl) for zh in range(n_row // row_step) for zl in range(n_col // col_step)]
    planes = [
        [flat(zh, x, zl, y * CORES + c) for x in range(row_step) for y in range(col_step // CORES)]
        for zh, zl in z
        for c in range(CORES)
    ]
    lines = [[flat(zh, x, zl, yc) for zh, zl in z] for x in range(row_step) for yc in range(col_step)]
    return planes, lines


def exchange(blocks, members):
    return lax.all_to_all(blocks, AXES, 0, 0, axis_index_groups=members, tiled=True)


def spread(chunk, members):
    return exchange(jnp.broadcast_to(chunk[None], (len(members[0]), *chunk.shape)), members)


def swap(block):
    count = lax.axis_size("col")
    return lax.ppermute(block, "col", [(i, i ^ 1) for i in range(count)])


def total(mine, other):
    planes, lines = groups(4, 8)
    mine = mine + swap(other)
    parts = exchange(mine.reshape(len(planes[0]), -1, LANES), planes)
    part = jnp.sum(spread(jnp.sum(parts, axis=0), lines), axis=0)
    mine = spread(part, planes).reshape(mine.shape)
    return mine, swap(mine)


def at(array, dim, start, stop):
    return lax.slice_in_dim(array, start, stop, axis=dim)


def padded(array, dim, low, size):
    pads = [(0, 0, 0)] * array.ndim
    pads[dim] = (low, size - low - array.shape[dim], 0)
    return lax.pad(array, jnp.float32(0), pads)


def on_device(object_field, probe, patterns, row_scales, positions, counts):
    modes, size = probe.shape[1], probe.shape[2]
    rim = size // 2
    rows, cols = object_field.shape[1:]
    tall, wide = rows + 2 * rim, cols + 2 * LANES
    margin = LANES - rim
    tables = [jnp.asarray(t) for t in dft_tables(size)]
    amplitude = patterns[0, 0].astype(jnp.float32) * row_scales[0, 0][..., None]
    starts, count = positions[0, 0], counts[0]

    low, high = neighbours(at(object_field, 1, 0, rim), at(object_field, 1, rows - rim, rows), "row")
    frame = jnp.concatenate([low, object_field, high], axis=1)
    low, high = neighbours(at(frame, 2, 0, LANES), at(frame, 2, cols - LANES, cols), "col")
    frame = jnp.concatenate([low, frame, high], axis=2)

    core = (lax.axis_index("col") % CORES).reshape(1)
    left, right = margin, LANES + cols + rim
    updates, mine, other = run_pass(starts, count, core, frame, probe, None, amplitude, tables, margin)
    means = total(mine, other)
    strips = at(updates, 2, left, right)
    low, high = neighbours(at(strips, 1, 0, 2 * rim), at(strips, 1, rows, tall), "row")
    strips = strips + padded(low, 1, 0, tall) + padded(high, 1, rows, tall)
    low, high = neighbours(at(strips, 2, 0, 2 * rim), at(strips, 2, cols, cols + 2 * rim), "col")
    strips = strips + padded(low, 2, 0, cols + 2 * rim) + padded(high, 2, cols, cols + 2 * rim)
    updates = padded(strips, 2, left, wide)
    at_row = lax.broadcasted_iota(jnp.int32, (1, tall, 1), 1) + (lax.axis_index("row") * rows - rim)
    at_col = lax.broadcasted_iota(jnp.int32, (1, 1, wide), 2) + (lax.axis_index("col") * cols - LANES)
    inside = (at_row >= 0) & (at_row < rows * lax.axis_size("row"))
    inside = inside & (at_col >= 0) & (at_col < cols * lax.axis_size("col"))
    frame = frame + jnp.where(inside, updates, 0.0)

    updates, mine, other, probe = run_pass(
        starts, count, core, frame, probe, means, amplitude, tables, margin
    )
    mine, other = total(mine, other)
    strips = at(updates, 2, left, right)
    low, high = neighbours(at(strips, 1, 0, rim), at(strips, 1, tall - rim, tall), "row")
    middle = at(strips, 1, rim, rim + rows)
    middle = middle + padded(low, 1, 0, rows) + padded(high, 1, rows - rim, rows)
    low, high = neighbours(at(middle, 2, 0, rim), at(middle, 2, rim + cols, cols + 2 * rim), "col")
    tile = at(middle, 2, rim, rim + cols)
    tile = tile + padded(low, 2, 0, cols) + padded(high, 2, cols - rim, cols)
    object_out = frame[:, rim : rim + rows, LANES : LANES + cols] + tile
    lower = jnp.where(core[0] == 0, mine, other)
    upper = jnp.where(core[0] == 0, other, mine)
    sums = jnp.concatenate([lower, upper]).reshape(-1, size, size)
    probe_out = probe + sums[: 2 * modes].reshape(probe.shape) / sums[2 * modes]
    return object_out, probe_out


def solution(mesh):
    placed = (
        P(None, "row", "col"),
        P(),
        P("row", "col", None, None, None),
        P("row", "col", None, None),
        P("row", "col", None, None),
        P("row", "col"),
    )
    return jax.shard_map(
        on_device,
        mesh=mesh,
        in_specs=placed,
        out_specs=(P(None, "row", "col"), P()),
        check_vma=False,
    )
```

```python
import functools

import numpy as np

import jax
import jax.numpy as jnp
from jax import lax
from jax.experimental import pallas as pl
from jax.experimental.pallas import tpu as pltpu
from jax.sharding import PartitionSpec as P


LANES = 128
SUBLANES = 8
CORES = 2
TOGETHER = 4


def dft_tables(length):
    index = np.arange(length)
    angle = (np.outer(index, index) % length) * (2.0 * np.pi / length)
    cosine = np.cos(angle) / np.sqrt(length)
    sine = np.sin(angle) / np.sqrt(length)
    forward = np.block([[cosine, -sine], [sine, cosine]]).astype(np.float32)
    high = forward.astype(jnp.bfloat16)
    low = (forward - high.astype(np.float32)).astype(jnp.bfloat16)
    return high, low, np.ascontiguousarray(high.T), np.ascontiguousarray(low.T)


def split(value):
    high = value.astype(jnp.bfloat16)
    low = (value - high.astype(jnp.float32)).astype(jnp.bfloat16)
    return high, low


def mm(left, right):
    return jnp.dot(left, right, preferred_element_type=jnp.float32)


def product(left, right):
    (lh, ll), (rh, rl) = left, right
    return mm(lh, rh) + (mm(lh, rl) + mm(ll, rh))


def pass_kernel(*refs, modes, size, margin, renew):
    if renew:
        starts, counts, core, frame, old_probe, mean_mine, mean_other, amplitude, *refs = refs
        fh, fl, ih, il, updates, mine, other, probe, sums = refs
        half_rows = mean_mine.shape[0]
        sums[pl.ds(pl.multiple_of(core[0] * half_rows, size), half_rows)] = mean_mine[...]
        sums[pl.ds(pl.multiple_of((1 - core[0]) * half_rows, size), half_rows)] = mean_other[...]
        weight = sums[pl.ds(2 * modes * size, size)]
        for part in range(2):
            for m in range(modes):
                step = sums[pl.ds((part * modes + m) * size, size)] / weight
                probe[part, m] = old_probe[part, m] + step
    else:
        starts, counts, core, frame, probe, amplitude, *refs = refs
        fh, fl, ih, il, updates, mine, other, sums = refs
    updates[...] = jnp.zeros_like(updates)
    sums[...] = jnp.zeros_like(sums)
    forward = (fh[...], fl[...])
    inverse = (ih[...], il[...])

    tall, wide = size + SUBLANES, 2 * size

    def window(p):
        row = starts[p, 0]
        col = starts[p, 1] + margin
        rows = pl.ds(pl.multiple_of(row // SUBLANES * SUBLANES, SUBLANES), tall)
        cols = pl.ds(pl.multiple_of(col // LANES * LANES, LANES), wide)
        return rows, cols, row % SUBLANES, col % LANES

    def cut(part, place):
        rows, cols, down, shift = place
        block = pltpu.roll(frame[part, rows, cols], lax.rem(wide - shift, wide), 1)[:, :size]
        return pltpu.roll(block, lax.rem(tall - down, tall), 0)[:size]

    def add(part, place, patch):
        rows, cols, down, shift = place
        patch = jnp.concatenate([patch, jnp.zeros((SUBLANES, size), jnp.float32)], axis=0)
        patch = pltpu.roll(patch, down, 0)
        patch = pltpu.roll(jnp.concatenate([patch, jnp.zeros_like(patch)], axis=1), shift, 1)
        updates[part, rows, cols] += patch

    def exits(patch):
        re, im = patch
        waves = []
        for m in range(modes):
            pr, pi = probe[0, m], probe[1, m]
            waves.append((pr * re - pi * im, pr * im + pi * re))
        return waves

    def along_rows(waves, table):
        stacked = jnp.concatenate([jnp.concatenate(w, axis=1) for w in waves], axis=0)
        return product(split(stacked), table)

    def side(half):
        blocks = [half[m * size : (m + 1) * size] for m in range(modes)]
        return jnp.concatenate(
            [jnp.concatenate([b[:, :size], b[:, size:]], axis=0) for b in blocks], axis=1
        )

    def scale(far, p):
        squares = far * far
        power = squares[:size] + squares[size:]
        intensity = power[:, :size]
        for m in range(1, modes):
            intensity = intensity + power[:, m * size : (m + 1) * size]
        factor = amplitude[p] / jnp.maximum(jnp.sqrt(intensity), 0.5)
        factor = jnp.concatenate([factor] * modes, axis=1)
        return far * jnp.concatenate([factor, factor], axis=0)

    def columns(half):
        return [
            (half[:size, m * size : (m + 1) * size], half[size:, m * size : (m + 1) * size])
            for m in range(modes)
        ]

    def several(step, carry):
        ps = [step * TOGETHER + k for k in range(TOGETHER)]
        ps = [jnp.minimum(p, last) for p in ps]
        live = [jnp.where(step * TOGETHER + k <= last, 1.0, 0.0) for k in range(TOGETHER)]
        places = [window(p) for p in ps]
        patches = [(cut(0, place), cut(1, place)) for place in places]
        halves = [along_rows(exits(patch), forward) for patch in patches]
        fars = [product(inverse, split(side(half))) for half in halves]
        halves = [product(forward, split(scale(far, p))) for far, p in zip(fars, ps)]
        backs = [along_rows(columns(half), inverse) for half in halves]
        differences = []
        for patch, back, on in zip(patches, backs, live):
            waves = exits(patch)
            differences.append(
                [
                    (
                        (back[m * size : (m + 1) * size, :size] - waves[m][0]) * on,
                        (back[m * size : (m + 1) * size, size:] - waves[m][1]) * on,
                    )
                    for m in range(modes)
                ]
            )
        for m in range(modes):
            g_re = g_im = None
            for (re, im), difference in zip(patches, differences):
                dr, di = difference[m]
                one_re, one_im = re * dr + im * di, re * di - im * dr
                g_re = one_re if g_re is None else g_re + one_re
                g_im = one_im if g_im is None else g_im + one_im
            sums[pl.ds(m * size, size)] += g_re
            sums[pl.ds((modes + m) * size, size)] += g_im
        weight = None
        for (re, im), on in zip(patches, live):
            one = (re * re + im * im) * on
            weight = one if weight is None else weight + one
        sums[pl.ds(2 * modes * size, size)] += weight
        for place, difference in zip(places, differences):
            total_re = total_im = None
            for m in range(modes):
                pr, pi = probe[0, m], probe[1, m]
                dr, di = difference[m]
                one_re, one_im = pr * dr + pi * di, pr * di - pi * dr
                total_re = one_re if m == 0 else total_re + one_re
                total_im = one_im if m == 0 else total_im + one_im
            add(0, place, total_re)
            add(1, place, total_im)
        return carry

    last = counts[0] - 1
    lax.fori_loop(0, (counts[0] + TOGETHER - 1) // TOGETHER, several, 0)
    strength = probe[0, 0] * probe[0, 0] + probe[1, 0] * probe[1, 0]
    for m in range(1, modes):
        strength = strength + probe[0, m] * probe[0, m] + probe[1, m] * probe[1, m]
    updates[...] = updates[...] / jnp.max(strength)
    half_rows = mine.shape[0]
    mine[...] = sums[pl.ds(pl.multiple_of(core[0] * half_rows, size), half_rows)]
    other[...] = sums[pl.ds(pl.multiple_of((1 - core[0]) * half_rows, size), half_rows)]


def run_pass(starts, count, core, frame, probe, means, amplitude, tables, margin):
    modes, size = probe.shape[1], probe.shape[2]
    renew = means is not None
    half_rows = (modes + 1) * size
    vmem = pl.BlockSpec(memory_space=pltpu.VMEM)
    smem = pl.BlockSpec(memory_space=pltpu.SMEM)
    flops = 24 * starts.shape[0] * modes * size * (2 * size) ** 2
    half = jax.ShapeDtypeStruct((half_rows, size), jnp.float32)
    shapes = [jax.ShapeDtypeStruct(frame.shape, jnp.float32), half, half]
    if renew:
        shapes.append(jax.ShapeDtypeStruct(probe.shape, jnp.float32))
    operands = [frame, probe, *(means or ()), amplitude, *tables]
    return pl.pallas_call(
        functools.partial(pass_kernel, modes=modes, size=size, margin=margin, renew=renew),
        out_shape=shapes,
        in_specs=[smem] * 3 + [vmem] * len(operands),
        out_specs=[vmem] * len(shapes),
        scratch_shapes=[pltpu.VMEM((2 * half_rows, size), jnp.float32)],
        cost_estimate=pl.CostEstimate(flops=flops, bytes_accessed=6 << 20, transcendentals=0),
        compiler_params=pltpu.CompilerParams(vmem_limit_bytes=48 << 20),
    )(starts, count, core, *operands)


def neighbours(low_strip, high_strip, axis):
    count = lax.axis_size(axis)
    odd = lax.axis_index(axis) % 2 == 1

    def meet(block, start):
        pairs = [(i, i + 1) for i in range(start, count - 1, 2)]
        return lax.ppermute(block, axis, pairs + [(j, i) for i, j in pairs])

    first = meet(jnp.where(odd, high_strip, low_strip), 1)
    second = meet(jnp.where(odd, low_strip, high_strip), 0)
    return jnp.where(odd, second, first), jnp.where(odd, first, second)


AXES = ("row", "col")


def groups(row_step, col_step):
    n_row, n_col = lax.axis_size("row"), lax.axis_size("col")

    def flat(zh, x, zl, yc):
        return (zh * row_step + x) * n_col + zl * col_step + yc

    z = [(zh, zl) for zh in range(n_row // row_step) for zl in range(n_col // col_step)]
    planes = [
        [flat(zh, x, zl, y * CORES + c) for x in range(row_step) for y in range(col_step // CORES)]
        for zh, zl in z
        for c in range(CORES)
    ]
    lines = [[flat(zh, x, zl, yc) for zh, zl in z] for x in range(row_step) for yc in range(col_step)]
    return planes, lines


def exchange(blocks, members):
    return lax.all_to_all(blocks, AXES, 0, 0, axis_index_groups=members, tiled=True)


def spread(chunk, members):
    return exchange(jnp.broadcast_to(chunk[None], (len(members[0]), *chunk.shape)), members)


def swap(block):
    count = lax.axis_size("col")
    return lax.ppermute(block, "col", [(i, i ^ 1) for i in range(count)])


def total(mine, other):
    planes, lines = groups(4, 8)
    mine = mine + swap(other)
    parts = exchange(mine.reshape(len(planes[0]), -1, LANES), planes)
    part = jnp.sum(spread(jnp.sum(parts, axis=0), lines), axis=0)
    mine = spread(part, planes).reshape(mine.shape)
    return mine, swap(mine)


def at(array, dim, start, stop):
    return lax.slice_in_dim(array, start, stop, axis=dim)


def padded(array, dim, low, size):
    pads = [(0, 0, 0)] * array.ndim
    pads[dim] = (low, size - low - array.shape[dim], 0)
    return lax.pad(array, jnp.float32(0), pads)


def on_device(object_field, probe, patterns, row_scales, positions, counts):
    modes, size = probe.shape[1], probe.shape[2]
    rim = size // 2
    rows, cols = object_field.shape[1:]
    tall, wide = rows + 2 * rim, cols + 2 * LANES
    margin = LANES - rim
    tables = [jnp.asarray(t) for t in dft_tables(size)]
    amplitude = patterns[0, 0].astype(jnp.float32) * row_scales[0, 0][..., None]
    starts, count = positions[0, 0], counts[0]

    low, high = neighbours(at(object_field, 1, 0, rim), at(object_field, 1, rows - rim, rows), "row")
    frame = jnp.concatenate([low, object_field, high], axis=1)
    low, high = neighbours(at(frame, 2, 0, LANES), at(frame, 2, cols - LANES, cols), "col")
    frame = jnp.concatenate([low, frame, high], axis=2)

    at_row = lax.broadcasted_iota(jnp.int32, (1, tall, 1), 1) + (lax.axis_index("row") * rows - rim)
    at_col = lax.broadcasted_iota(jnp.int32, (1, 1, wide), 2) + (lax.axis_index("col") * cols - LANES)
    inside = (at_row >= 0) & (at_row < rows * lax.axis_size("row"))
    inside = inside & (at_col >= 0) & (at_col < cols * lax.axis_size("col"))
    core = (lax.axis_index("col") % CORES).reshape(1)
    left, right = margin, LANES + cols + rim
    updates, mine, other = run_pass(starts, count, core, frame, probe, None, amplitude, tables, margin)
    means = total(mine, other)
    strips = at(updates, 2, left, right)
    low, high = neighbours(at(strips, 2, 0, 2 * rim), at(strips, 2, cols, cols + 2 * rim), "col")
    strips = strips + padded(low, 2, 0, cols + 2 * rim) + padded(high, 2, cols, cols + 2 * rim)
    low, high = neighbours(at(strips, 1, 0, 2 * rim), at(strips, 1, rows, tall), "row")
    strips = strips + padded(low, 1, 0, tall) + padded(high, 1, rows, tall)
    updates = padded(strips, 2, left, wide)
    frame = frame + jnp.where(inside, updates, 0.0)

    updates, mine, other, probe = run_pass(
        starts, count, core, frame, probe, means, amplitude, tables, margin
    )
    mine, other = total(mine, other)
    strips = at(updates, 2, left, right)
    low, high = neighbours(at(strips, 2, 0, rim), at(strips, 2, rim + cols, cols + 2 * rim), "col")
    middle = at(strips, 2, rim, rim + cols)
    middle = middle + padded(low, 2, 0, cols) + padded(high, 2, cols - rim, cols)
    low, high = neighbours(at(middle, 1, 0, rim), at(middle, 1, tall - rim, tall), "row")
    tile = at(middle, 1, rim, rim + rows)
    tile = tile + padded(low, 1, 0, rows) + padded(high, 1, rows - rim, rows)
    object_out = frame[:, rim : rim + rows, LANES : LANES + cols] + tile
    lower = jnp.where(core[0] == 0, mine, other)
    upper = jnp.where(core[0] == 0, other, mine)
    sums = jnp.concatenate([lower, upper]).reshape(-1, size, size)
    probe_out = probe + sums[: 2 * modes].reshape(probe.shape) / sums[2 * modes]
    return object_out, probe_out


def solution(mesh):
    placed = (
        P(None, "row", "col"),
        P(),
        P("row", "col", None, None, None),
        P("row", "col", None, None),
        P("row", "col", None, None),
        P("row", "col"),
    )
    return jax.shard_map(
        on_device,
        mesh=mesh,
        in_specs=placed,
        out_specs=(P(None, "row", "col"), P()),
        check_vma=False,
    )
```

```python
import functools

import numpy as np

import jax
import jax.numpy as jnp
from jax import lax
from jax.experimental import pallas as pl
from jax.experimental.pallas import tpu as pltpu
from jax.sharding import PartitionSpec as P


LANES = 128
SUBLANES = 8
CORES = 2
TOGETHER = 4


def dft_tables(length):
    index = np.arange(length)
    angle = (np.outer(index, index) % length) * (2.0 * np.pi / length)
    cosine = np.cos(angle) / np.sqrt(length)
    sine = np.sin(angle) / np.sqrt(length)
    forward = np.block([[cosine, -sine], [sine, cosine]]).astype(np.float32)
    high = forward.astype(jnp.bfloat16)
    low = (forward - high.astype(np.float32)).astype(jnp.bfloat16)
    return high, low, np.ascontiguousarray(high.T), np.ascontiguousarray(low.T)


def split(value):
    high = value.astype(jnp.bfloat16)
    low = (value - high.astype(jnp.float32)).astype(jnp.bfloat16)
    return high, low


def mm(left, right):
    return jnp.dot(left, right, preferred_element_type=jnp.float32)


def product(left, right):
    (lh, ll), (rh, rl) = left, right
    return mm(lh, rh) + (mm(lh, rl) + mm(ll, rh))


def pass_kernel(*refs, modes, size, margin, renew):
    if renew:
        starts, counts, core, frame, old_probe, mean_mine, mean_other, amplitude, *refs = refs
        fh, fl, ih, il, updates, mine, other, probe, sums = refs
        half_rows = mean_mine.shape[0]
        sums[pl.ds(pl.multiple_of(core[0] * half_rows, size), half_rows)] = mean_mine[...]
        sums[pl.ds(pl.multiple_of((1 - core[0]) * half_rows, size), half_rows)] = mean_other[...]
        weight = sums[pl.ds(2 * modes * size, size)]
        for part in range(2):
            for m in range(modes):
                step = sums[pl.ds((part * modes + m) * size, size)] / weight
                probe[part, m] = old_probe[part, m] + step
    else:
        starts, counts, core, frame, probe, amplitude, *refs = refs
        fh, fl, ih, il, updates, mine, other, sums = refs
    updates[...] = jnp.zeros_like(updates)
    sums[...] = jnp.zeros_like(sums)
    forward = (fh[...], fl[...])
    inverse = (ih[...], il[...])

    tall, wide = size + SUBLANES, 2 * size

    def window(p):
        row = starts[p, 0]
        col = starts[p, 1] + margin
        rows = pl.ds(pl.multiple_of(row // SUBLANES * SUBLANES, SUBLANES), tall)
        cols = pl.ds(pl.multiple_of(col // LANES * LANES, LANES), wide)
        return rows, cols, row % SUBLANES, col % LANES

    def cut(part, place):
        rows, cols, down, shift = place
        block = pltpu.roll(frame[part, rows, cols], lax.rem(wide - shift, wide), 1)[:, :size]
        return pltpu.roll(block, lax.rem(tall - down, tall), 0)[:size]

    def add(part, place, patch):
        rows, cols, down, shift = place
        patch = jnp.concatenate([patch, jnp.zeros((SUBLANES, size), jnp.float32)], axis=0)
        patch = pltpu.roll(patch, down, 0)
        patch = pltpu.roll(jnp.concatenate([patch, jnp.zeros_like(patch)], axis=1), shift, 1)
        updates[part, rows, cols] += patch

    def exits(patch):
        re, im = patch
        waves = []
        for m in range(modes):
            pr, pi = probe[0, m], probe[1, m]
            waves.append((pr * re - pi * im, pr * im + pi * re))
        return waves

    def along_rows(waves, table):
        stacked = jnp.concatenate([jnp.concatenate(w, axis=1) for w in waves], axis=0)
        return product(split(stacked), table)

    def side(half):
        blocks = [half[m * size : (m + 1) * size] for m in range(modes)]
        return jnp.concatenate(
            [jnp.concatenate([b[:, :size], b[:, size:]], axis=0) for b in blocks], axis=1
        )

    def scale(far, p):
        squares = far * far
        power = squares[:size] + squares[size:]
        intensity = power[:, :size]
        for m in range(1, modes):
            intensity = intensity + power[:, m * size : (m + 1) * size]
        factor = amplitude[p] / jnp.maximum(jnp.sqrt(intensity), 0.5)
        factor = jnp.concatenate([factor] * modes, axis=1)
        return far * jnp.concatenate([factor, factor], axis=0)

    def columns(half):
        return [
            (half[:size, m * size : (m + 1) * size], half[size:, m * size : (m + 1) * size])
            for m in range(modes)
        ]

    def several(step, carry):
        ps = [step * TOGETHER + k for k in range(TOGETHER)]
        ps = [jnp.minimum(p, last) for p in ps]
        live = [jnp.where(step * TOGETHER + k <= last, 1.0, 0.0) for k in range(TOGETHER)]
        places = [window(p) for p in ps]
        patches = [(cut(0, place), cut(1, place)) for place in places]
        halves = [along_rows(exits(patch), forward) for patch in patches]
        fars = [product(inverse, split(side(half))) for half in halves]
        halves = [product(forward, split(scale(far, p))) for far, p in zip(fars, ps)]
        backs = [along_rows(columns(half), inverse) for half in halves]
        differences = []
        for patch, back, on in zip(patches, backs, live):
            waves = exits(patch)
            differences.append(
                [
                    (
                        (back[m * size : (m + 1) * size, :size] - waves[m][0]) * on,
                        (back[m * size : (m + 1) * size, size:] - waves[m][1]) * on,
                    )
                    for m in range(modes)
                ]
            )
        for m in range(modes):
            g_re = g_im = None
            for (re, im), difference in zip(patches, differences):
                dr, di = difference[m]
                one_re, one_im = re * dr + im * di, re * di - im * dr
                g_re = one_re if g_re is None else g_re + one_re
                g_im = one_im if g_im is None else g_im + one_im
            sums[pl.ds(m * size, size)] += g_re
            sums[pl.ds((modes + m) * size, size)] += g_im
        weight = None
        for (re, im), on in zip(patches, live):
            one = (re * re + im * im) * on
            weight = one if weight is None else weight + one
        sums[pl.ds(2 * modes * size, size)] += weight
        for place, difference in zip(places, differences):
            total_re = total_im = None
            for m in range(modes):
                pr, pi = probe[0, m], probe[1, m]
                dr, di = difference[m]
                one_re, one_im = pr * dr + pi * di, pr * di - pi * dr
                total_re = one_re if m == 0 else total_re + one_re
                total_im = one_im if m == 0 else total_im + one_im
            add(0, place, total_re)
            add(1, place, total_im)
        return carry

    last = counts[0] - 1
    lax.fori_loop(0, (counts[0] + TOGETHER - 1) // TOGETHER, several, 0)
    strength = probe[0, 0] * probe[0, 0] + probe[1, 0] * probe[1, 0]
    for m in range(1, modes):
        strength = strength + probe[0, m] * probe[0, m] + probe[1, m] * probe[1, m]
    updates[...] = updates[...] / jnp.max(strength)
    half_rows = mine.shape[0]
    mine[...] = sums[pl.ds(pl.multiple_of(core[0] * half_rows, size), half_rows)]
    other[...] = sums[pl.ds(pl.multiple_of((1 - core[0]) * half_rows, size), half_rows)]


def run_pass(starts, count, core, frame, probe, means, amplitude, tables, margin):
    modes, size = probe.shape[1], probe.shape[2]
    renew = means is not None
    half_rows = (modes + 1) * size
    vmem = pl.BlockSpec(memory_space=pltpu.VMEM)
    smem = pl.BlockSpec(memory_space=pltpu.SMEM)
    flops = 24 * starts.shape[0] * modes * size * (2 * size) ** 2
    half = jax.ShapeDtypeStruct((half_rows, size), jnp.float32)
    shapes = [jax.ShapeDtypeStruct(frame.shape, jnp.float32), half, half]
    if renew:
        shapes.append(jax.ShapeDtypeStruct(probe.shape, jnp.float32))
    operands = [frame, probe, *(means or ()), amplitude, *tables]
    return pl.pallas_call(
        functools.partial(pass_kernel, modes=modes, size=size, margin=margin, renew=renew),
        out_shape=shapes,
        in_specs=[smem] * 3 + [vmem] * len(operands),
        out_specs=[vmem] * len(shapes),
        scratch_shapes=[pltpu.VMEM((2 * half_rows, size), jnp.float32)],
        cost_estimate=pl.CostEstimate(flops=flops, bytes_accessed=6 << 20, transcendentals=0),
        compiler_params=pltpu.CompilerParams(vmem_limit_bytes=48 << 20),
    )(starts, count, core, *operands)


def neighbours(low_strip, high_strip, axis):
    count = lax.axis_size(axis)
    odd = lax.axis_index(axis) % 2 == 1

    def meet(block, start):
        pairs = [(i, i + 1) for i in range(start, count - 1, 2)]
        return lax.ppermute(block, axis, pairs + [(j, i) for i, j in pairs])

    first = meet(jnp.where(odd, high_strip, low_strip), 1)
    second = meet(jnp.where(odd, low_strip, high_strip), 0)
    return jnp.where(odd, second, first), jnp.where(odd, first, second)


AXES = ("row", "col")


def groups(row_step, col_step):
    n_row, n_col = lax.axis_size("row"), lax.axis_size("col")

    def flat(zh, x, zl, yc):
        return (zh * row_step + x) * n_col + zl * col_step + yc

    z = [(zh, zl) for zh in range(n_row // row_step) for zl in range(n_col // col_step)]
    planes = [
        [flat(zh, x, zl, y * CORES + c) for x in range(row_step) for y in range(col_step // CORES)]
        for zh, zl in z
        for c in range(CORES)
    ]
    lines = [[flat(zh, x, zl, yc) for zh, zl in z] for x in range(row_step) for yc in range(col_step)]
    return planes, lines


def exchange(blocks, members):
    return lax.all_to_all(blocks, AXES, 0, 0, axis_index_groups=members, tiled=True)


def spread(chunk, members):
    return exchange(jnp.broadcast_to(chunk[None], (len(members[0]), *chunk.shape)), members)


def swap(block):
    count = lax.axis_size("col")
    return lax.ppermute(block, "col", [(i, i ^ 1) for i in range(count)])


def total(mine, other):
    planes, lines = groups(4, 8)
    mine = mine + swap(other)
    parts = exchange(mine.reshape(len(planes[0]), -1, LANES), planes)
    part = jnp.sum(spread(jnp.sum(parts, axis=0), lines), axis=0)
    mine = spread(part, planes).reshape(mine.shape)
    return mine, swap(mine)


def at(array, dim, start, stop):
    return lax.slice_in_dim(array, start, stop, axis=dim)


def padded(array, dim, low, size):
    pads = [(0, 0, 0)] * array.ndim
    pads[dim] = (low, size - low - array.shape[dim], 0)
    return lax.pad(array, jnp.float32(0), pads)


def on_device(object_field, probe, patterns, row_scales, positions, counts):
    modes, size = probe.shape[1], probe.shape[2]
    rim = size // 2
    rows, cols = object_field.shape[1:]
    tall, wide = rows + 2 * rim, cols + 2 * LANES
    margin = LANES - rim
    tables = [jnp.asarray(t) for t in dft_tables(size)]
    amplitude = patterns[0, 0].astype(jnp.float32) * row_scales[0, 0][..., None]
    starts, count = positions[0, 0], counts[0]

    low, high = neighbours(at(object_field, 1, 0, rim), at(object_field, 1, rows - rim, rows), "row")
    frame = jnp.concatenate([low, object_field, high], axis=1)
    low, high = neighbours(at(frame, 2, 0, LANES), at(frame, 2, cols - LANES, cols), "col")
    frame = jnp.concatenate([low, frame, high], axis=2)

    at_row = lax.broadcasted_iota(jnp.int32, (1, tall, 1), 1) + (lax.axis_index("row") * rows - rim)
    at_col = lax.broadcasted_iota(jnp.int32, (1, 1, wide), 2) + (lax.axis_index("col") * cols - LANES)
    inside = (at_row >= 0) & (at_row < rows * lax.axis_size("row"))
    inside = inside & (at_col >= 0) & (at_col < cols * lax.axis_size("col"))
    core = (lax.axis_index("col") % CORES).reshape(1)
    left, right = margin, LANES + cols + rim

    def folded(updates):
        strips = at(updates, 2, left, right)
        low, high = neighbours(at(strips, 1, 0, rim), at(strips, 1, tall - rim, tall), "row")
        middle = at(strips, 1, rim, rim + rows)
        return middle + padded(low, 1, 0, rows) + padded(high, 1, rows - rim, rows)

    updates, mine, other = run_pass(starts, count, core, frame, probe, None, amplitude, tables, margin)
    means = total(mine, other)
    middle = folded(updates)
    low, high = neighbours(at(middle, 2, 0, 2 * rim), at(middle, 2, cols, cols + 2 * rim), "col")
    middle = middle + padded(low, 2, 0, cols + 2 * rim) + padded(high, 2, cols, cols + 2 * rim)
    low, high = neighbours(at(middle, 1, 0, rim), at(middle, 1, rows - rim, rows), "row")
    whole = jnp.concatenate([low, middle, high], axis=1)
    frame = frame + jnp.where(inside, padded(whole, 2, left, wide), 0.0)

    updates, mine, other, probe = run_pass(
        starts, count, core, frame, probe, means, amplitude, tables, margin
    )
    mine, other = total(mine, other)
    middle = folded(updates)
    low, high = neighbours(at(middle, 2, 0, rim), at(middle, 2, rim + cols, cols + 2 * rim), "col")
    tile = at(middle, 2, rim, rim + cols)
    tile = tile + padded(low, 2, 0, cols) + padded(high, 2, cols - rim, cols)
    object_out = frame[:, rim : rim + rows, LANES : LANES + cols] + tile
    lower = jnp.where(core[0] == 0, mine, other)
    upper = jnp.where(core[0] == 0, other, mine)
    sums = jnp.concatenate([lower, upper]).reshape(-1, size, size)
    probe_out = probe + sums[: 2 * modes].reshape(probe.shape) / sums[2 * modes]
    return object_out, probe_out


def solution(mesh):
    placed = (
        P(None, "row", "col"),
        P(),
        P("row", "col", None, None, None),
        P("row", "col", None, None),
        P("row", "col", None, None),
        P("row", "col"),
    )
    return jax.shard_map(
        on_device,
        mesh=mesh,
        in_specs=placed,
        out_specs=(P(None, "row", "col"), P()),
        check_vma=False,
    )
```

```python
import functools

import numpy as np

import jax
import jax.numpy as jnp
from jax import lax
from jax.experimental import pallas as pl
from jax.experimental.pallas import tpu as pltpu
from jax.sharding import PartitionSpec as P


LANES = 128
SUBLANES = 8
CORES = 2
TOGETHER = 4


def dft_tables(length):
    index = np.arange(length)
    angle = (np.outer(index, index) % length) * (2.0 * np.pi / length)
    cosine = np.cos(angle) / np.sqrt(length)
    sine = np.sin(angle) / np.sqrt(length)
    forward = np.block([[cosine, -sine], [sine, cosine]]).astype(np.float32)
    high = forward.astype(jnp.bfloat16)
    low = (forward - high.astype(np.float32)).astype(jnp.bfloat16)
    return high, low, np.ascontiguousarray(high.T), np.ascontiguousarray(low.T)


def split(value):
    high = value.astype(jnp.bfloat16)
    low = (value - high.astype(jnp.float32)).astype(jnp.bfloat16)
    return high, low


def mm(left, right):
    return jnp.dot(left, right, preferred_element_type=jnp.float32)


def product(left, right):
    (lh, ll), (rh, rl) = left, right
    return mm(lh, rh) + (mm(lh, rl) + mm(ll, rh))


def pass_kernel(*refs, modes, size, margin, renew):
    if renew:
        starts, counts, core, frame, old_probe, mean_mine, mean_other, amplitude, *refs = refs
        fh, fl, ih, il, updates, mine, other, probe, sums = refs
        half_rows = mean_mine.shape[0]
        sums[pl.ds(pl.multiple_of(core[0] * half_rows, size), half_rows)] = mean_mine[...]
        sums[pl.ds(pl.multiple_of((1 - core[0]) * half_rows, size), half_rows)] = mean_other[...]
        weight = sums[pl.ds(2 * modes * size, size)]
        for part in range(2):
            for m in range(modes):
                step = sums[pl.ds((part * modes + m) * size, size)] / weight
                probe[part, m] = old_probe[part, m] + step
    else:
        starts, counts, core, frame, probe, amplitude, *refs = refs
        fh, fl, ih, il, updates, mine, other, sums = refs
    updates[...] = jnp.zeros_like(updates)
    sums[...] = jnp.zeros_like(sums)
    forward = (fh[...], fl[...])
    inverse = (ih[...], il[...])

    tall, wide = size + SUBLANES, 2 * size

    def window(p):
        row = starts[p, 0]
        col = starts[p, 1] + margin
        rows = pl.ds(pl.multiple_of(row // SUBLANES * SUBLANES, SUBLANES), tall)
        cols = pl.ds(pl.multiple_of(col // LANES * LANES, LANES), wide)
        return rows, cols, row % SUBLANES, col % LANES

    def cut(part, place):
        rows, cols, down, shift = place
        block = pltpu.roll(frame[part, rows, cols], lax.rem(wide - shift, wide), 1)[:, :size]
        return pltpu.roll(block, lax.rem(tall - down, tall), 0)[:size]

    def add(part, place, patch):
        rows, cols, down, shift = place
        patch = jnp.concatenate([patch, jnp.zeros((SUBLANES, size), jnp.float32)], axis=0)
        patch = pltpu.roll(patch, down, 0)
        patch = pltpu.roll(jnp.concatenate([patch, jnp.zeros_like(patch)], axis=1), shift, 1)
        updates[part, rows, cols] += patch

    def exits(patch):
        re, im = patch
        waves = []
        for m in range(modes):
            pr, pi = probe[0, m], probe[1, m]
            waves.append((pr * re - pi * im, pr * im + pi * re))
        return waves

    def along_rows(waves, table):
        stacked = jnp.concatenate([jnp.concatenate(w, axis=1) for w in waves], axis=0)
        return product(split(stacked), table)

    def side(half):
        blocks = [half[m * size : (m + 1) * size] for m in range(modes)]
        return jnp.concatenate(
            [jnp.concatenate([b[:, :size], b[:, size:]], axis=0) for b in blocks], axis=1
        )

    def scale(far, p):
        squares = far * far
        power = squares[:size] + squares[size:]
        intensity = power[:, :size]
        for m in range(1, modes):
            intensity = intensity + power[:, m * size : (m + 1) * size]
        factor = amplitude[p] / jnp.maximum(jnp.sqrt(intensity), 0.5)
        factor = jnp.concatenate([factor] * modes, axis=1)
        return far * jnp.concatenate([factor, factor], axis=0)

    def columns(half):
        return [
            (half[:size, m * size : (m + 1) * size], half[size:, m * size : (m + 1) * size])
            for m in range(modes)
        ]

    def several(step, carry):
        ps = [step * TOGETHER + k for k in range(TOGETHER)]
        ps = [jnp.minimum(p, last) for p in ps]
        live = [jnp.where(step * TOGETHER + k <= last, 1.0, 0.0) for k in range(TOGETHER)]
        places = [window(p) for p in ps]
        patches = [(cut(0, place), cut(1, place)) for place in places]
        halves = [along_rows(exits(patch), forward) for patch in patches]
        fars = [product(inverse, split(side(half))) for half in halves]
        halves = [product(forward, split(scale(far, p))) for far, p in zip(fars, ps)]
        backs = [along_rows(columns(half), inverse) for half in halves]
        differences = []
        for patch, back, on in zip(patches, backs, live):
            waves = exits(patch)
            differences.append(
                [
                    (
                        (back[m * size : (m + 1) * size, :size] - waves[m][0]) * on,
                        (back[m * size : (m + 1) * size, size:] - waves[m][1]) * on,
                    )
                    for m in range(modes)
                ]
            )
        for m in range(modes):
            g_re = g_im = None
            for (re, im), difference in zip(patches, differences):
                dr, di = difference[m]
                one_re, one_im = re * dr + im * di, re * di - im * dr
                g_re = one_re if g_re is None else g_re + one_re
                g_im = one_im if g_im is None else g_im + one_im
            sums[pl.ds(m * size, size)] += g_re
            sums[pl.ds((modes + m) * size, size)] += g_im
        weight = None
        for (re, im), on in zip(patches, live):
            one = (re * re + im * im) * on
            weight = one if weight is None else weight + one
        sums[pl.ds(2 * modes * size, size)] += weight
        for place, difference in zip(places, differences):
            total_re = total_im = None
            for m in range(modes):
                pr, pi = probe[0, m], probe[1, m]
                dr, di = difference[m]
                one_re, one_im = pr * dr + pi * di, pr * di - pi * dr
                total_re = one_re if m == 0 else total_re + one_re
                total_im = one_im if m == 0 else total_im + one_im
            add(0, place, total_re)
            add(1, place, total_im)
        return carry

    last = counts[0] - 1
    lax.fori_loop(0, (counts[0] + TOGETHER - 1) // TOGETHER, several, 0)
    strength = probe[0, 0] * probe[0, 0] + probe[1, 0] * probe[1, 0]
    for m in range(1, modes):
        strength = strength + probe[0, m] * probe[0, m] + probe[1, m] * probe[1, m]
    updates[...] = updates[...] / jnp.max(strength)
    half_rows = mine.shape[0]
    mine[...] = sums[pl.ds(pl.multiple_of(core[0] * half_rows, size), half_rows)]
    other[...] = sums[pl.ds(pl.multiple_of((1 - core[0]) * half_rows, size), half_rows)]


def run_pass(starts, count, core, frame, probe, means, amplitude, tables, margin):
    modes, size = probe.shape[1], probe.shape[2]
    renew = means is not None
    half_rows = (modes + 1) * size
    vmem = pl.BlockSpec(memory_space=pltpu.VMEM)
    smem = pl.BlockSpec(memory_space=pltpu.SMEM)
    flops = 24 * starts.shape[0] * modes * size * (2 * size) ** 2
    half = jax.ShapeDtypeStruct((half_rows, size), jnp.float32)
    shapes = [jax.ShapeDtypeStruct(frame.shape, jnp.float32), half, half]
    if renew:
        shapes.append(jax.ShapeDtypeStruct(probe.shape, jnp.float32))
    operands = [frame, probe, *(means or ()), amplitude, *tables]
    return pl.pallas_call(
        functools.partial(pass_kernel, modes=modes, size=size, margin=margin, renew=renew),
        out_shape=shapes,
        in_specs=[smem] * 3 + [vmem] * len(operands),
        out_specs=[vmem] * len(shapes),
        scratch_shapes=[pltpu.VMEM((2 * half_rows, size), jnp.float32)],
        cost_estimate=pl.CostEstimate(flops=flops, bytes_accessed=6 << 20, transcendentals=0),
        compiler_params=pltpu.CompilerParams(vmem_limit_bytes=48 << 20),
    )(starts, count, core, *operands)


def neighbours(low_strip, high_strip, axis, apart=False):
    count = lax.axis_size(axis)
    odd = lax.axis_index(axis) % 2 == 1

    def meet(block, pairs):
        return lax.ppermute(block, axis, pairs + [(j, i) for i, j in pairs])

    middle = [(count // 2 - 1, count // 2)]
    pairs = [(i, i + 1) for i in range(1, count - 1, 2)]
    block = jnp.where(odd, high_strip, low_strip)
    first = meet(block, middle if apart else pairs)
    if apart:
        first = first + meet(block, [pair for pair in pairs if pair not in middle])
    second = meet(
        jnp.where(odd, low_strip, high_strip), [(i, i + 1) for i in range(0, count - 1, 2)]
    )
    return jnp.where(odd, second, first), jnp.where(odd, first, second)


AXES = ("row", "col")


def groups(row_step, col_step):
    n_row, n_col = lax.axis_size("row"), lax.axis_size("col")

    def flat(zh, x, zl, yc):
        return (zh * row_step + x) * n_col + zl * col_step + yc

    z = [(zh, zl) for zh in range(n_row // row_step) for zl in range(n_col // col_step)]
    planes = [
        [flat(zh, x, zl, y * CORES + c) for x in range(row_step) for y in range(col_step // CORES)]
        for zh, zl in z
        for c in range(CORES)
    ]
    lines = [[flat(zh, x, zl, yc) for zh, zl in z] for x in range(row_step) for yc in range(col_step)]
    return planes, lines


def exchange(blocks, members):
    return lax.all_to_all(blocks, AXES, 0, 0, axis_index_groups=members, tiled=True)


def spread(chunk, members):
    return exchange(jnp.broadcast_to(chunk[None], (len(members[0]), *chunk.shape)), members)


def swap(block):
    count = lax.axis_size("col")
    return lax.ppermute(block, "col", [(i, i ^ 1) for i in range(count)])


def total(mine, other):
    planes, lines = groups(4, 8)
    mine = mine + swap(other)
    parts = exchange(mine.reshape(len(planes[0]), -1, LANES), planes)
    part = jnp.sum(spread(jnp.sum(parts, axis=0), lines), axis=0)
    mine = spread(part, planes).reshape(mine.shape)
    return mine, swap(mine)


def at(array, dim, start, stop):
    return lax.slice_in_dim(array, start, stop, axis=dim)


def padded(array, dim, low, size):
    pads = [(0, 0, 0)] * array.ndim
    pads[dim] = (low, size - low - array.shape[dim], 0)
    return lax.pad(array, jnp.float32(0), pads)


def on_device(object_field, probe, patterns, row_scales, positions, counts):
    modes, size = probe.shape[1], probe.shape[2]
    rim = size // 2
    rows, cols = object_field.shape[1:]
    tall, wide = rows + 2 * rim, cols + 2 * LANES
    margin = LANES - rim
    tables = [jnp.asarray(t) for t in dft_tables(size)]
    amplitude = patterns[0, 0].astype(jnp.float32) * row_scales[0, 0][..., None]
    starts, count = positions[0, 0], counts[0]

    low, high = neighbours(at(object_field, 1, 0, rim), at(object_field, 1, rows - rim, rows), "row")
    frame = jnp.concatenate([low, object_field, high], axis=1)
    low, high = neighbours(at(frame, 2, 0, LANES), at(frame, 2, cols - LANES, cols), "col")
    frame = jnp.concatenate([low, frame, high], axis=2)

    core = (lax.axis_index("col") % CORES).reshape(1)
    left, right = margin, LANES + cols + rim
    updates, mine, other = run_pass(starts, count, core, frame, probe, None, amplitude, tables, margin)
    means = total(mine, other)
    strips = at(updates, 2, left, right)
    low, high = neighbours(at(strips, 1, 0, 2 * rim), at(strips, 1, rows, tall), "row", True)
    strips = strips + padded(low, 1, 0, tall) + padded(high, 1, rows, tall)
    low, high = neighbours(at(strips, 2, 0, 2 * rim), at(strips, 2, cols, cols + 2 * rim), "col")
    strips = strips + padded(low, 2, 0, cols + 2 * rim) + padded(high, 2, cols, cols + 2 * rim)
    updates = padded(strips, 2, left, wide)
    at_row = lax.broadcasted_iota(jnp.int32, (1, tall, 1), 1) + (lax.axis_index("row") * rows - rim)
    at_col = lax.broadcasted_iota(jnp.int32, (1, 1, wide), 2) + (lax.axis_index("col") * cols - LANES)
    inside = (at_row >= 0) & (at_row < rows * lax.axis_size("row"))
    inside = inside & (at_col >= 0) & (at_col < cols * lax.axis_size("col"))
    frame = frame + jnp.where(inside, updates, 0.0)

    updates, mine, other, probe = run_pass(
        starts, count, core, frame, probe, means, amplitude, tables, margin
    )
    mine, other = total(mine, other)
    strips = at(updates, 2, left, right)
    low, high = neighbours(at(strips, 1, 0, rim), at(strips, 1, tall - rim, tall), "row", True)
    middle = at(strips, 1, rim, rim + rows)
    middle = middle + padded(low, 1, 0, rows) + padded(high, 1, rows - rim, rows)
    low, high = neighbours(at(middle, 2, 0, rim), at(middle, 2, rim + cols, cols + 2 * rim), "col")
    tile = at(middle, 2, rim, rim + cols)
    tile = tile + padded(low, 2, 0, cols) + padded(high, 2, cols - rim, cols)
    object_out = frame[:, rim : rim + rows, LANES : LANES + cols] + tile
    lower = jnp.where(core[0] == 0, mine, other)
    upper = jnp.where(core[0] == 0, other, mine)
    sums = jnp.concatenate([lower, upper]).reshape(-1, size, size)
    probe_out = probe + sums[: 2 * modes].reshape(probe.shape) / sums[2 * modes]
    return object_out, probe_out


def solution(mesh):
    placed = (
        P(None, "row", "col"),
        P(),
        P("row", "col", None, None, None),
        P("row", "col", None, None),
        P("row", "col", None, None),
        P("row", "col"),
    )
    return jax.shard_map(
        on_device,
        mesh=mesh,
        in_specs=placed,
        out_specs=(P(None, "row", "col"), P()),
        check_vma=False,
    )
```

```python
import functools

import numpy as np

import jax
import jax.numpy as jnp
from jax import lax
from jax.experimental import pallas as pl
from jax.experimental.pallas import tpu as pltpu
from jax.sharding import PartitionSpec as P


LANES = 128
SUBLANES = 8
CORES = 2
TOGETHER = 4


def dft_tables(length):
    index = np.arange(length)
    angle = (np.outer(index, index) % length) * (2.0 * np.pi / length)
    cosine = np.cos(angle) / np.sqrt(length)
    sine = np.sin(angle) / np.sqrt(length)
    forward = np.block([[cosine, -sine], [sine, cosine]]).astype(np.float32)
    high = forward.astype(jnp.bfloat16)
    low = (forward - high.astype(np.float32)).astype(jnp.bfloat16)
    return high, low, np.ascontiguousarray(high.T), np.ascontiguousarray(low.T)


def split(value):
    high = value.astype(jnp.bfloat16)
    low = (value - high.astype(jnp.float32)).astype(jnp.bfloat16)
    return high, low


def mm(left, right):
    return jnp.dot(left, right, preferred_element_type=jnp.float32)


def product(left, right):
    (lh, ll), (rh, rl) = left, right
    return mm(lh, rh) + (mm(lh, rl) + mm(ll, rh))


def pass_kernel(*refs, modes, size, margin, renew):
    if renew:
        starts, counts, core, frame, old_probe, mean_mine, mean_other, amplitude, *refs = refs
        fh, fl, ih, il, updates, mine, other, probe, sums = refs
        half_rows = mean_mine.shape[0]
        sums[pl.ds(pl.multiple_of(core[0] * half_rows, size), half_rows)] = mean_mine[...]
        sums[pl.ds(pl.multiple_of((1 - core[0]) * half_rows, size), half_rows)] = mean_other[...]
        weight = sums[pl.ds(2 * modes * size, size)]
        for part in range(2):
            for m in range(modes):
                step = sums[pl.ds((part * modes + m) * size, size)] / weight
                probe[part, m] = old_probe[part, m] + step
    else:
        starts, counts, core, frame, probe, amplitude, *refs = refs
        fh, fl, ih, il, updates, mine, other, sums = refs
    updates[...] = jnp.zeros_like(updates)
    sums[...] = jnp.zeros_like(sums)
    forward = (fh[...], fl[...])
    inverse = (ih[...], il[...])

    tall, wide = size + SUBLANES, 2 * size

    def window(p):
        row = starts[p, 0]
        col = starts[p, 1] + margin
        rows = pl.ds(pl.multiple_of(row // SUBLANES * SUBLANES, SUBLANES), tall)
        cols = pl.ds(pl.multiple_of(col // LANES * LANES, LANES), wide)
        return rows, cols, row % SUBLANES, col % LANES

    def cut(part, place):
        rows, cols, down, shift = place
        block = pltpu.roll(frame[part, rows, cols], lax.rem(wide - shift, wide), 1)[:, :size]
        return pltpu.roll(block, lax.rem(tall - down, tall), 0)[:size]

    def add(part, place, patch):
        rows, cols, down, shift = place
        patch = jnp.concatenate([patch, jnp.zeros((SUBLANES, size), jnp.float32)], axis=0)
        patch = pltpu.roll(patch, down, 0)
        patch = pltpu.roll(jnp.concatenate([patch, jnp.zeros_like(patch)], axis=1), shift, 1)
        updates[part, rows, cols] += patch

    def exits(patch):
        re, im = patch
        waves = []
        for m in range(modes):
            pr, pi = probe[0, m], probe[1, m]
            waves.append((pr * re - pi * im, pr * im + pi * re))
        return waves

    def along_rows(waves, table):
        stacked = jnp.concatenate([jnp.concatenate(w, axis=1) for w in waves], axis=0)
        return product(split(stacked), table)

    def side(half):
        blocks = [half[m * size : (m + 1) * size] for m in range(modes)]
        return jnp.concatenate(
            [jnp.concatenate([b[:, :size], b[:, size:]], axis=0) for b in blocks], axis=1
        )

    def scale(far, p):
        squares = far * far
        power = squares[:size] + squares[size:]
        intensity = power[:, :size]
        for m in range(1, modes):
            intensity = intensity + power[:, m * size : (m + 1) * size]
        factor = amplitude[p] / jnp.maximum(jnp.sqrt(intensity), 0.5)
        factor = jnp.concatenate([factor] * modes, axis=1)
        return far * jnp.concatenate([factor, factor], axis=0)

    def columns(half):
        return [
            (half[:size, m * size : (m + 1) * size], half[size:, m * size : (m + 1) * size])
            for m in range(modes)
        ]

    def several(step, carry):
        ps = [step * TOGETHER + k for k in range(TOGETHER)]
        ps = [jnp.minimum(p, last) for p in ps]
        live = [jnp.where(step * TOGETHER + k <= last, 1.0, 0.0) for k in range(TOGETHER)]
        places = [window(p) for p in ps]
        patches = [(cut(0, place), cut(1, place)) for place in places]
        halves = [along_rows(exits(patch), forward) for patch in patches]
        fars = [product(inverse, split(side(half))) for half in halves]
        halves = [product(forward, split(scale(far, p))) for far, p in zip(fars, ps)]
        backs = [along_rows(columns(half), inverse) for half in halves]
        differences = []
        for patch, back, on in zip(patches, backs, live):
            waves = exits(patch)
            differences.append(
                [
                    (
                        (back[m * size : (m + 1) * size, :size] - waves[m][0]) * on,
                        (back[m * size : (m + 1) * size, size:] - waves[m][1]) * on,
                    )
                    for m in range(modes)
                ]
            )
        for m in range(modes):
            g_re = g_im = None
            for (re, im), difference in zip(patches, differences):
                dr, di = difference[m]
                one_re, one_im = re * dr + im * di, re * di - im * dr
                g_re = one_re if g_re is None else g_re + one_re
                g_im = one_im if g_im is None else g_im + one_im
            sums[pl.ds(m * size, size)] += g_re
            sums[pl.ds((modes + m) * size, size)] += g_im
        weight = None
        for (re, im), on in zip(patches, live):
            one = (re * re + im * im) * on
            weight = one if weight is None else weight + one
        sums[pl.ds(2 * modes * size, size)] += weight
        for place, difference in zip(places, differences):
            total_re = total_im = None
            for m in range(modes):
                pr, pi = probe[0, m], probe[1, m]
                dr, di = difference[m]
                one_re, one_im = pr * dr + pi * di, pr * di - pi * dr
                total_re = one_re if m == 0 else total_re + one_re
                total_im = one_im if m == 0 else total_im + one_im
            add(0, place, total_re)
            add(1, place, total_im)
        return carry

    last = counts[0] - 1
    lax.fori_loop(0, (counts[0] + TOGETHER - 1) // TOGETHER, several, 0)
    strength = probe[0, 0] * probe[0, 0] + probe[1, 0] * probe[1, 0]
    for m in range(1, modes):
        strength = strength + probe[0, m] * probe[0, m] + probe[1, m] * probe[1, m]
    updates[...] = updates[...] / jnp.max(strength)
    half_rows = mine.shape[0]
    mine[...] = sums[pl.ds(pl.multiple_of(core[0] * half_rows, size), half_rows)]
    other[...] = sums[pl.ds(pl.multiple_of((1 - core[0]) * half_rows, size), half_rows)]


def run_pass(starts, count, core, frame, probe, means, amplitude, tables, margin):
    modes, size = probe.shape[1], probe.shape[2]
    renew = means is not None
    half_rows = (modes + 1) * size
    vmem = pl.BlockSpec(memory_space=pltpu.VMEM)
    smem = pl.BlockSpec(memory_space=pltpu.SMEM)
    flops = 24 * starts.shape[0] * modes * size * (2 * size) ** 2
    half = jax.ShapeDtypeStruct((half_rows, size), jnp.float32)
    shapes = [jax.ShapeDtypeStruct(frame.shape, jnp.float32), half, half]
    if renew:
        shapes.append(jax.ShapeDtypeStruct(probe.shape, jnp.float32))
    operands = [frame, probe, *(means or ()), amplitude, *tables]
    return pl.pallas_call(
        functools.partial(pass_kernel, modes=modes, size=size, margin=margin, renew=renew),
        out_shape=shapes,
        in_specs=[smem] * 3 + [vmem] * len(operands),
        out_specs=[vmem] * len(shapes),
        scratch_shapes=[pltpu.VMEM((2 * half_rows, size), jnp.float32)],
        cost_estimate=pl.CostEstimate(flops=flops, bytes_accessed=6 << 20, transcendentals=0),
        compiler_params=pltpu.CompilerParams(vmem_limit_bytes=48 << 20),
    )(starts, count, core, *operands)


def neighbours(low_strip, high_strip, axis):
    count = lax.axis_size(axis)
    odd = lax.axis_index(axis) % 2 == 1

    def meet(block, start):
        pairs = [(i, i + 1) for i in range(start, count - 1, 2)]
        return lax.ppermute(block, axis, pairs + [(j, i) for i, j in pairs])

    first = meet(jnp.where(odd, high_strip, low_strip), 1)
    second = meet(jnp.where(odd, low_strip, high_strip), 0)
    return jnp.where(odd, second, first), jnp.where(odd, first, second)


AXES = ("row", "col")


def groups(row_step, col_step):
    n_row, n_col = lax.axis_size("row"), lax.axis_size("col")

    def flat(zh, x, zl, yc):
        return (zh * row_step + x) * n_col + zl * col_step + yc

    z = [(zh, zl) for zh in range(n_row // row_step) for zl in range(n_col // col_step)]
    planes = [
        [flat(zh, x, zl, y * CORES + c) for x in range(row_step) for y in range(col_step // CORES)]
        for zh, zl in z
        for c in range(CORES)
    ]
    lines = [[flat(zh, x, zl, yc) for zh, zl in z] for x in range(row_step) for yc in range(col_step)]
    return planes, lines


def exchange(blocks, members):
    return lax.all_to_all(blocks, AXES, 0, 0, axis_index_groups=members, tiled=True)


def spread(chunk, members):
    return exchange(jnp.broadcast_to(chunk[None], (len(members[0]), *chunk.shape)), members)


def swap(block):
    count = lax.axis_size("col")
    return lax.ppermute(block, "col", [(i, i ^ 1) for i in range(count)])


def total(mine, other):
    planes, lines = groups(4, 8)
    mine = mine + swap(other)
    parts = exchange(mine.reshape(len(planes[0]), -1, LANES), planes)
    part = jnp.sum(spread(jnp.sum(parts, axis=0), lines), axis=0)
    mine = spread(part, planes).reshape(mine.shape)
    return mine, swap(mine)


def at(array, dim, start, stop):
    return lax.slice_in_dim(array, start, stop, axis=dim)


def padded(array, dim, low, size):
    pads = [(0, 0, 0)] * array.ndim
    pads[dim] = (low, size - low - array.shape[dim], 0)
    return lax.pad(array, jnp.float32(0), pads)


def on_device(object_field, probe, patterns, row_scales, positions, counts):
    modes, size = probe.shape[1], probe.shape[2]
    rim = size // 2
    rows, cols = object_field.shape[1:]
    tall, wide = rows + 2 * rim, cols + 2 * LANES
    margin = LANES - rim
    tables = [jnp.asarray(t) for t in dft_tables(size)]
    amplitude = patterns[0, 0].astype(jnp.float32) * row_scales[0, 0][..., None]
    starts, count = positions[0, 0], counts[0]

    low, high = neighbours(at(object_field, 1, 0, rim), at(object_field, 1, rows - rim, rows), "row")
    frame = jnp.concatenate([low, object_field, high], axis=1)
    low, high = neighbours(at(frame, 2, 0, LANES), at(frame, 2, cols - LANES, cols), "col")
    frame = jnp.concatenate([low, frame, high], axis=2)

    core = (lax.axis_index("col") % CORES).reshape(1)
    left, right = margin, LANES + cols + rim
    updates, mine, other = run_pass(starts, count, core, frame, probe, None, amplitude, tables, margin)
    means = total(mine, other)
    strips = at(updates, 2, left, right)
    low, high = neighbours(at(strips, 1, 0, 2 * rim), at(strips, 1, rows, tall), "row")
    strips = strips + padded(low, 1, 0, tall) + padded(high, 1, rows, tall)
    low, high = neighbours(at(strips, 2, 0, 2 * rim), at(strips, 2, cols, cols + 2 * rim), "col")
    strips = strips + padded(low, 2, 0, cols + 2 * rim) + padded(high, 2, cols, cols + 2 * rim)
    updates = padded(strips, 2, left, wide)
    at_row = lax.broadcasted_iota(jnp.int32, (1, tall, 1), 1) + (lax.axis_index("row") * rows - rim)
    at_col = lax.broadcasted_iota(jnp.int32, (1, 1, wide), 2) + (lax.axis_index("col") * cols - LANES)
    inside = (at_row >= 0) & (at_row < rows * lax.axis_size("row"))
    inside = inside & (at_col >= 0) & (at_col < cols * lax.axis_size("col"))
    frame = frame + jnp.where(inside, updates, 0.0)

    updates, mine, other, probe = run_pass(
        starts, count, core, frame, probe, means, amplitude, tables, margin
    )
    mine, other = total(mine, other)
    strips = at(updates, 2, left, right)
    low, high = neighbours(at(strips, 1, 0, rim), at(strips, 1, tall - rim, tall), "row")
    middle = at(strips, 1, rim, rim + rows)
    middle = middle + padded(low, 1, 0, rows) + padded(high, 1, rows - rim, rows)
    low, high = neighbours(at(middle, 2, 0, rim), at(middle, 2, rim + cols, cols + 2 * rim), "col")
    tile = at(middle, 2, rim, rim + cols)
    tile = tile + padded(low, 2, 0, cols) + padded(high, 2, cols - rim, cols)
    object_out = frame[:, rim : rim + rows, LANES : LANES + cols] + tile
    lower = jnp.where(core[0] == 0, mine, other)
    upper = jnp.where(core[0] == 0, other, mine)
    sums = jnp.concatenate([lower, upper]).reshape(-1, size, size)
    probe_out = probe + sums[: 2 * modes].reshape(probe.shape) / sums[2 * modes]
    return object_out, probe_out


def solution(mesh):
    placed = (
        P(None, "row", "col"),
        P(),
        P("row", "col", None, None, None),
        P("row", "col", None, None),
        P("row", "col", None, None),
        P("row", "col"),
    )
    return jax.shard_map(
        on_device,
        mesh=mesh,
        in_specs=placed,
        out_specs=(P(None, "row", "col"), P()),
        check_vma=False,
    )
```

```python
import functools

import numpy as np

import jax
import jax.numpy as jnp
from jax import lax
from jax.experimental import pallas as pl
from jax.experimental.pallas import tpu as pltpu
from jax.sharding import PartitionSpec as P


LANES = 128
SUBLANES = 8
CORES = 2
TOGETHER = 4


def dft_tables(length):
    index = np.arange(length)
    angle = (np.outer(index, index) % length) * (2.0 * np.pi / length)
    cosine = np.cos(angle) / np.sqrt(length)
    sine = np.sin(angle) / np.sqrt(length)
    forward = np.block([[cosine, -sine], [sine, cosine]]).astype(np.float32)
    high = forward.astype(jnp.bfloat16)
    low = (forward - high.astype(np.float32)).astype(jnp.bfloat16)
    return high, low, np.ascontiguousarray(high.T), np.ascontiguousarray(low.T)


def split(value):
    high = value.astype(jnp.bfloat16)
    low = (value - high.astype(jnp.float32)).astype(jnp.bfloat16)
    return high, low


def mm(left, right):
    return jnp.dot(left, right, preferred_element_type=jnp.float32)


def product(left, right):
    (lh, ll), (rh, rl) = left, right
    return mm(lh, rh) + (mm(lh, rl) + mm(ll, rh))


def pass_kernel(*refs, modes, size, margin, renew):
    if renew:
        starts, counts, core, frame, old_probe, mean_mine, mean_other, amplitude, *refs = refs
        fh, fl, ih, il, updates, mine, other, probe, sums = refs
        half_rows = mean_mine.shape[0]
        sums[pl.ds(pl.multiple_of(core[0] * half_rows, size), half_rows)] = mean_mine[...]
        sums[pl.ds(pl.multiple_of((1 - core[0]) * half_rows, size), half_rows)] = mean_other[...]
        weight = sums[pl.ds(2 * modes * size, size)]
        for part in range(2):
            for m in range(modes):
                step = sums[pl.ds((part * modes + m) * size, size)] / weight
                probe[part, m] = old_probe[part, m] + step
    else:
        starts, counts, core, frame, probe, amplitude, *refs = refs
        fh, fl, ih, il, updates, mine, other, sums = refs
    updates[...] = jnp.zeros_like(updates)
    sums[...] = jnp.zeros_like(sums)
    forward = (fh[...], fl[...])
    inverse = (ih[...], il[...])

    tall, wide = size + SUBLANES, 2 * size

    def window(p):
        row = starts[p, 0]
        col = starts[p, 1] + margin
        rows = pl.ds(pl.multiple_of(row // SUBLANES * SUBLANES, SUBLANES), tall)
        cols = pl.ds(pl.multiple_of(col // LANES * LANES, LANES), wide)
        return rows, cols, row % SUBLANES, col % LANES

    def cut(part, place):
        rows, cols, down, shift = place
        block = pltpu.roll(frame[part, rows, cols], lax.rem(wide - shift, wide), 1)[:, :size]
        return pltpu.roll(block, lax.rem(tall - down, tall), 0)[:size]

    def add(part, place, patch):
        rows, cols, down, shift = place
        patch = jnp.concatenate([patch, jnp.zeros((SUBLANES, size), jnp.float32)], axis=0)
        patch = pltpu.roll(patch, down, 0)
        patch = pltpu.roll(jnp.concatenate([patch, jnp.zeros_like(patch)], axis=1), shift, 1)
        updates[part, rows, cols] += patch

    def exits(patch):
        re, im = patch
        waves = []
        for m in range(modes):
            pr, pi = probe[0, m], probe[1, m]
            waves.append((pr * re - pi * im, pr * im + pi * re))
        return waves

    def along_rows(waves, table):
        stacked = jnp.concatenate([jnp.concatenate(w, axis=1) for w in waves], axis=0)
        return product(split(stacked), table)

    def side(half):
        blocks = [half[m * size : (m + 1) * size] for m in range(modes)]
        return jnp.concatenate(
            [jnp.concatenate([b[:, :size], b[:, size:]], axis=0) for b in blocks], axis=1
        )

    def scale(far, p):
        squares = far * far
        power = squares[:size] + squares[size:]
        intensity = power[:, :size]
        for m in range(1, modes):
            intensity = intensity + power[:, m * size : (m + 1) * size]
        factor = amplitude[p] / jnp.maximum(jnp.sqrt(intensity), 0.5)
        factor = jnp.concatenate([factor] * modes, axis=1)
        return far * jnp.concatenate([factor, factor], axis=0)

    def columns(half):
        return [
            (half[:size, m * size : (m + 1) * size], half[size:, m * size : (m + 1) * size])
            for m in range(modes)
        ]

    def several(step, carry):
        ps = [step * TOGETHER + k for k in range(TOGETHER)]
        ps = [jnp.minimum(p, last) for p in ps]
        live = [jnp.where(step * TOGETHER + k <= last, 1.0, 0.0) for k in range(TOGETHER)]
        places = [window(p) for p in ps]
        patches = [(cut(0, place), cut(1, place)) for place in places]
        halves = [along_rows(exits(patch), forward) for patch in patches]
        fars = [product(inverse, split(side(half))) for half in halves]
        halves = [product(forward, split(scale(far, p))) for far, p in zip(fars, ps)]
        backs = [along_rows(columns(half), inverse) for half in halves]
        differences = []
        for patch, back, on in zip(patches, backs, live):
            waves = exits(patch)
            differences.append(
                [
                    (
                        (back[m * size : (m + 1) * size, :size] - waves[m][0]) * on,
                        (back[m * size : (m + 1) * size, size:] - waves[m][1]) * on,
                    )
                    for m in range(modes)
                ]
            )
        for m in range(modes):
            g_re = g_im = None
            for (re, im), difference in zip(patches, differences):
                dr, di = difference[m]
                one_re, one_im = re * dr + im * di, re * di - im * dr
                g_re = one_re if g_re is None else g_re + one_re
                g_im = one_im if g_im is None else g_im + one_im
            sums[pl.ds(m * size, size)] += g_re
            sums[pl.ds((modes + m) * size, size)] += g_im
        weight = None
        for (re, im), on in zip(patches, live):
            one = (re * re + im * im) * on
            weight = one if weight is None else weight + one
        sums[pl.ds(2 * modes * size, size)] += weight
        for place, difference in zip(places, differences):
            total_re = total_im = None
            for m in range(modes):
                pr, pi = probe[0, m], probe[1, m]
                dr, di = difference[m]
                one_re, one_im = pr * dr + pi * di, pr * di - pi * dr
                total_re = one_re if m == 0 else total_re + one_re
                total_im = one_im if m == 0 else total_im + one_im
            add(0, place, total_re)
            add(1, place, total_im)
        return carry

    last = counts[0] - 1
    lax.fori_loop(0, (counts[0] + TOGETHER - 1) // TOGETHER, several, 0)
    strength = probe[0, 0] * probe[0, 0] + probe[1, 0] * probe[1, 0]
    for m in range(1, modes):
        strength = strength + probe[0, m] * probe[0, m] + probe[1, m] * probe[1, m]
    updates[...] = updates[...] / jnp.max(strength)
    half_rows = mine.shape[0]
    mine[...] = sums[pl.ds(pl.multiple_of(core[0] * half_rows, size), half_rows)]
    other[...] = sums[pl.ds(pl.multiple_of((1 - core[0]) * half_rows, size), half_rows)]


def run_pass(starts, count, core, frame, probe, means, amplitude, tables, margin):
    modes, size = probe.shape[1], probe.shape[2]
    renew = means is not None
    half_rows = (modes + 1) * size
    vmem = pl.BlockSpec(memory_space=pltpu.VMEM)
    smem = pl.BlockSpec(memory_space=pltpu.SMEM)
    flops = 24 * starts.shape[0] * modes * size * (2 * size) ** 2
    half = jax.ShapeDtypeStruct((half_rows, size), jnp.float32)
    shapes = [jax.ShapeDtypeStruct(frame.shape, jnp.float32), half, half]
    if renew:
        shapes.append(jax.ShapeDtypeStruct(probe.shape, jnp.float32))
    operands = [frame, probe, *(means or ()), amplitude, *tables]
    return pl.pallas_call(
        functools.partial(pass_kernel, modes=modes, size=size, margin=margin, renew=renew),
        out_shape=shapes,
        in_specs=[smem] * 3 + [vmem] * len(operands),
        out_specs=[vmem] * len(shapes),
        scratch_shapes=[pltpu.VMEM((2 * half_rows, size), jnp.float32)],
        cost_estimate=pl.CostEstimate(flops=flops, bytes_accessed=6 << 20, transcendentals=0),
        compiler_params=pltpu.CompilerParams(vmem_limit_bytes=48 << 20),
    )(starts, count, core, *operands)


def neighbours(low_strip, high_strip, axis):
    count = lax.axis_size(axis)
    odd = lax.axis_index(axis) % 2 == 1

    def meet(block, start):
        pairs = [(i, i + 1) for i in range(start, count - 1, 2)]
        return lax.ppermute(block, axis, pairs + [(j, i) for i, j in pairs])

    first = meet(jnp.where(odd, high_strip, low_strip), 1)
    second = meet(jnp.where(odd, low_strip, high_strip), 0)
    return jnp.where(odd, second, first), jnp.where(odd, first, second)


AXES = ("row", "col")


def groups(row_step, col_step):
    n_row, n_col = lax.axis_size("row"), lax.axis_size("col")

    def flat(zh, x, zl, yc):
        return (zh * row_step + x) * n_col + zl * col_step + yc

    z = [(zh, zl) for zh in range(n_row // row_step) for zl in range(n_col // col_step)]
    planes = [
        [flat(zh, x, zl, y * CORES + c) for x in range(row_step) for y in range(col_step // CORES)]
        for zh, zl in z
        for c in range(CORES)
    ]
    lines = [[flat(zh, x, zl, yc) for zh, zl in z] for x in range(row_step) for yc in range(col_step)]
    return planes, lines


def exchange(blocks, members):
    return lax.all_to_all(blocks, AXES, 0, 0, axis_index_groups=members, tiled=True)


def spread(chunk, members):
    return exchange(jnp.broadcast_to(chunk[None], (len(members[0]), *chunk.shape)), members)


def swap(block):
    count = lax.axis_size("col")
    return lax.ppermute(block, "col", [(i, i ^ 1) for i in range(count)])


def total(mine, other):
    planes, lines = groups(4, 8)
    mine = mine + swap(other)
    parts = exchange(mine.reshape(len(planes[0]), -1, LANES), planes)
    part = jnp.sum(spread(jnp.sum(parts, axis=0), lines), axis=0)
    mine = spread(part, planes).reshape(mine.shape)
    return mine, swap(mine)


def at(array, dim, start, stop):
    return lax.slice_in_dim(array, start, stop, axis=dim)


def padded(array, dim, low, size):
    pads = [(0, 0, 0)] * array.ndim
    pads[dim] = (low, size - low - array.shape[dim], 0)
    return lax.pad(array, jnp.float32(0), pads)


def on_device(object_field, probe, patterns, row_scales, positions, counts):
    modes, size = probe.shape[1], probe.shape[2]
    rim = size // 2
    rows, cols = object_field.shape[1:]
    tall, wide = rows + 2 * rim, cols + 2 * LANES
    margin = LANES - rim
    tables = [jnp.asarray(t) for t in dft_tables(size)]
    amplitude = patterns[0, 0].astype(jnp.float32) * row_scales[0, 0][..., None]
    starts, count = positions[0, 0], counts[0]

    low, high = neighbours(at(object_field, 1, 0, rim), at(object_field, 1, rows - rim, rows), "row")
    frame = jnp.concatenate([low, object_field, high], axis=1)
    low, high = neighbours(at(frame, 2, 0, LANES), at(frame, 2, cols - LANES, cols), "col")
    frame = jnp.concatenate([low, frame, high], axis=2)

    core = (lax.axis_index("col") % CORES).reshape(1)
    left, right = margin, LANES + cols + rim
    updates, mine, other = run_pass(starts, count, core, frame, probe, None, amplitude, tables, margin)
    means = total(mine, other)
    strips = at(updates, 2, left, right)
    low, high = neighbours(at(strips, 1, 0, 2 * rim), at(strips, 1, rows, tall), "row")
    strips = strips + padded(low, 1, 0, tall) + padded(high, 1, rows, tall)
    low, high = neighbours(at(strips, 2, 0, 2 * rim), at(strips, 2, cols, cols + 2 * rim), "col")
    at_row = lax.broadcasted_iota(jnp.int32, (1, tall, 1), 1) + (lax.axis_index("row") * rows - rim)
    at_col = lax.broadcasted_iota(jnp.int32, (1, 1, wide), 2) + (lax.axis_index("col") * cols - LANES)
    inside = (at_row >= 0) & (at_row < rows * lax.axis_size("row"))
    inside = inside & (at_col >= 0) & (at_col < cols * lax.axis_size("col"))
    early = frame + jnp.where(inside, padded(strips, 2, left, wide), 0.0)
    early, low, high = lax.optimization_barrier((early, low, high))
    late = padded(low, 2, left, wide) + padded(high, 2, left + cols, wide)
    frame = early + jnp.where(inside, late, 0.0)

    updates, mine, other, probe = run_pass(
        starts, count, core, frame, probe, means, amplitude, tables, margin
    )
    mine, other = total(mine, other)
    strips = at(updates, 2, left, right)
    low, high = neighbours(at(strips, 1, 0, rim), at(strips, 1, tall - rim, tall), "row")
    middle = at(strips, 1, rim, rim + rows)
    middle = middle + padded(low, 1, 0, rows) + padded(high, 1, rows - rim, rows)
    low, high = neighbours(at(middle, 2, 0, rim), at(middle, 2, rim + cols, cols + 2 * rim), "col")
    tile = at(middle, 2, rim, rim + cols)
    tile = tile + padded(low, 2, 0, cols) + padded(high, 2, cols - rim, cols)
    object_out = frame[:, rim : rim + rows, LANES : LANES + cols] + tile
    lower = jnp.where(core[0] == 0, mine, other)
    upper = jnp.where(core[0] == 0, other, mine)
    sums = jnp.concatenate([lower, upper]).reshape(-1, size, size)
    probe_out = probe + sums[: 2 * modes].reshape(probe.shape) / sums[2 * modes]
    return object_out, probe_out


def solution(mesh):
    placed = (
        P(None, "row", "col"),
        P(),
        P("row", "col", None, None, None),
        P("row", "col", None, None),
        P("row", "col", None, None),
        P("row", "col"),
    )
    return jax.shard_map(
        on_device,
        mesh=mesh,
        in_specs=placed,
        out_specs=(P(None, "row", "col"), P()),
        check_vma=False,
    )
```
